128 devices in a mesh: seq: 32 (over y, x_lo, z), tp: 4 (over x_hi, core).
Axes of the slice: x: 4 (x_hi: 2, x_lo: 2; x = x_hi * 2 + x_lo), y: 4, z: 4, core: 2. Of those that a mesh axis runs over, the one named last changes fastest.
Arguments:
- x_part: bfloat16 [4, 4096, 8192], P(None, 'seq', 'tp'), may hold values from -6 to 6
- z_part: bfloat16 [4, 4096, 8192], P(None, 'seq', 'tp'), may hold values from -6 to 6
- conv_weight: bfloat16 [4, 8192], replicated, may hold values from -3 to 3
- conv_bias: bfloat16 [8192], replicated, may hold values from -0.5 to 0.5
- dt_in_weight: bfloat16 [8192, 256], replicated, may hold values from -0.0625 to 0.0625
- bc_weight: bfloat16 [8192, 32], replicated, may hold values from -0.125 to 0.125
- dt_proj: bfloat16 [256, 8192], replicated, may hold values from -0.375 to 0.375
- dt_bias: float32 [8192], replicated, may hold values from -9 to -2
- a_log: float32 [16, 8192], replicated, may hold values from -3 to 2.5
- d_skip: float32 [8192], replicated, may hold values from 0.5 to 1.5
- lengths: int32 [4], replicated, may hold values from 1024 to 4096, as said below
- token_ids: int32 [3, 4], replicated, may hold values from 0 to 65535
- embedding: bfloat16 [65536, 4096], P(('seq', 'tp')), may hold values from -6 to 6
- dec_in_weight: bfloat16 [2, 4096, 4, 2048], P(None, None, None, 'seq'), may hold values from -0.09375 to 0.09375
- out_weight: bfloat16 [4, 2048, 4096], P(None, 'seq'), may hold values from -0.0625 to 0.0625
Outputs:
- mixed_out: bfloat16 [4, 4096, 8192], P(None, 'seq', 'tp')
- decoded: bfloat16 [3, 4, 4096], P(None, 'tp')
The draws below stay inside these ranges and needn't reach their ends.
Inputs may be any that keep to these rules, and one draw needn't show every extreme that they name: `lengths`: some sequence is exactly 4096 long, and none is shorter than 1024.
All inputs are finite; a program needn't handle non-finite values.
Results may differ from the reference program's by a relative error of at most 0.008.
Values may be sent and summed in bfloat16 or wider, within the bound.
A program may use at most 192 MiB of HBM per device.

```python
import math
from functools import partial
import jax
import jax.numpy as jnp
import numpy as np
from jax import lax

D = 4096
E = 8192
NST = 16
RANK = 256
KCONV = 4
VOCAB = 65536
ROWS = 4
DEC = 3
L = 4096
ECH = 2048
TGROUPS = 4


def draw_lengths(key, part):
    first_key, second_key = jax.random.split(key)
    spread = jax.random.randint(first_key, (ROWS,), L // 4, L + 1)
    chosen = jax.random.randint(second_key, (), 0, ROWS)
    return jnp.where(jnp.arange(ROWS) == chosen, L, spread).astype(jnp.int32)


def set_ends(entries, rng, least, high):
    shape = entries.shape
    spot = [jax.random.randint(jax.random.fold_in(rng, axis), (), 0, shape[axis]) for axis in range(len(shape))]
    entries = entries.at[tuple(spot)].set(least)
    longest = shape.index(max(shape))
    spot[longest] = (spot[longest] + 1) % shape[longest]
    return entries.at[tuple(spot)].set(high)


def block_scale(stream_key, dims, pieces, low, high):
    def one(dim, parts):
        steps = jax.random.uniform(jax.random.fold_in(jax.random.fold_in(stream_key, 6), dim), (parts,), jnp.float32, low / len(pieces), high / len(pieces))
        return jnp.repeat(jnp.exp(steps), dims[dim] // parts).reshape((-1,) + (1,) * (len(dims) - dim - 1))

    loudness = one(*pieces[0])
    for cut in pieces[1:]:
        loudness = loudness * one(*cut)
    return loudness


def cumulative_ranks(amount, lean):
    loads = [(1 << 20) // math.isqrt(standing ** lean) + 1 for standing in range(1, amount + 1)]
    scale = 1 + sum(loads) // (1 << 30)
    return np.cumsum(np.array([max(1, weight // scale) for weight in loads]))


def ranked(key, shape, amount, lean):
    grid = cumulative_ranks(amount, lean)
    ticket = jax.random.randint(jax.random.fold_in(key, 1), shape, 0, int(grid[amount - 1]))
    rank = jnp.searchsorted(jnp.asarray(grid, jnp.int32), ticket, side="right")
    return jax.random.permutation(jax.random.fold_in(key, 2), amount)[rank].astype(jnp.int32)


def gaussian(rng, dims, width, reach, cuts=(), dtype=jnp.bfloat16):
    drawn = jax.random.normal(rng, dims, jnp.float32) * width
    if len(cuts) > 0:
        drawn = block_scale(rng, dims, cuts, -0.22, 0.18) * drawn
    return jnp.clip(drawn, min=-reach, max=reach).astype(dtype)


def setup_inputs(seed: int = 0) -> dict:
    key_of = jax.random.split(jax.random.key(seed), 16)
    return {
        "x_part": gaussian(key_of[0], (ROWS, L, E), 1.0, 6.0, ((1, 32), (2, 4))),
        "z_part": gaussian(key_of[1], (ROWS, L, E), 1.0, 6.0, ((1, 32), (2, 4))),
        "conv_weight": gaussian(key_of[2], (KCONV, E), 0.5, 3.0),
        "conv_bias": jnp.clip(jax.random.uniform(key_of[3], (E,), jnp.float32, -0.5, 0.5), -0.5, 0.5).astype(jnp.bfloat16),
        "dt_in_weight": gaussian(key_of[4], (E, RANK), E ** -0.5, 0.0625),
        "bc_weight": gaussian(key_of[5], (E, 2 * NST), (E // 4) ** -0.5, 0.125),
        "dt_proj": gaussian(key_of[6], (RANK, E), RANK ** -0.5, 0.375),
        "dt_bias": jnp.clip(jax.random.uniform(key_of[7], (E,), jnp.float32, -9.0, -2.0), -9.0, -2.0),
        "a_log": jnp.clip(jax.random.uniform(key_of[8], (NST, E), jnp.float32, -3.0, 2.5), -3.0, 2.5),
        "d_skip": jnp.clip(jax.random.uniform(key_of[9], (E,), jnp.float32, 0.5, 1.5), 0.5, 1.5),
        "lengths": draw_lengths(jax.random.fold_in(key_of[15], 71), 0),
        "token_ids": set_ends(ranked(key_of[11], (DEC, ROWS), VOCAB, 2), jax.random.fold_in(key_of[11], 3), 0, VOCAB - 1).astype(jnp.int32),
        "embedding": gaussian(key_of[12], (VOCAB, D), 1.0, 6.0, ((0, 128),)),
        "dec_in_weight": gaussian(key_of[13], (2, D, TGROUPS, ECH), D ** -0.5, 0.09375, ((3, 32),)),
        "out_weight": gaussian(key_of[14], (TGROUPS, ECH, D), E ** -0.5, 0.0625, ((1, 32),)),
    }


EPSILON = 1e-06

def advance_state(decay_rate, ssm_state, step_inputs):
    step_dt, step_x, step_b, step_c = step_inputs
    ssm_state = jnp.exp(step_dt[:, None, :] * decay_rate[None]) * ssm_state + (step_dt * step_x)[:, None, :] * step_b[:, :, None]
    return (ssm_state, lax.optimization_barrier(jnp.sum(ssm_state * step_c[:, :, None], axis=1)))

def rms_scale(values):
    return values * lax.rsqrt(lax.optimization_barrier(jnp.mean(values * values, axis=-1, keepdims=True)) + EPSILON)

def normalize(values):
    return rms_scale(values).astype(jnp.bfloat16)

def reference(x_part, z_part, conv_weight, conv_bias, dt_in_weight, bc_weight, dt_proj, dt_bias, a_log, d_skip, lengths, token_ids, embedding, dec_in_weight, out_weight):
    float_type = jnp.float32
    half_type = jnp.bfloat16
    x_float = x_part.astype(float_type)
    padded = jnp.pad(x_float, ((0, 0), (KCONV - 1, 0), (0, 0)))
    conv_sum = conv_bias.astype(float_type)
    for tap_index in range(KCONV):
        conv_sum = conv_sum + conv_weight[tap_index].astype(float_type) * padded[:, tap_index:tap_index + L, :]
    xconv = jax.nn.silu(conv_sum).astype(half_type)
    flat_conv = xconv.reshape(ROWS * L, E)
    dt_low = jnp.dot(flat_conv, dt_in_weight, preferred_element_type=float_type)
    bc_all = jnp.dot(flat_conv, bc_weight, preferred_element_type=float_type).reshape(ROWS, L, 2 * NST)
    b_in = rms_scale(bc_all[:, :, :NST])
    c_out = rms_scale(bc_all[:, :, NST:])
    valid_mask = (jnp.arange(L).astype(jnp.int32)[None, :] < lengths[:, None]).astype(float_type)
    step_size = jax.nn.softplus(jnp.dot(normalize(dt_low), dt_proj, preferred_element_type=float_type) + dt_bias)
    step_size = step_size.reshape(ROWS, L, E) * valid_mask[:, :, None]
    decay_rate = -jnp.exp(a_log)
    x_conv_float = xconv.astype(float_type)
    scan_inputs = (jnp.moveaxis(step_size, 1, 0), jnp.moveaxis(x_conv_float, 1, 0), jnp.moveaxis(b_in, 1, 0), jnp.moveaxis(c_out, 1, 0))
    final_state, outputs = lax.scan(partial(advance_state, decay_rate), jnp.zeros((ROWS, NST, E), float_type), scan_inputs)
    outputs = jnp.moveaxis(outputs, 0, 1)
    mixed_out = ((outputs + d_skip * x_conv_float) * jax.nn.silu(z_part.astype(float_type)) * valid_mask[:, :, None]).astype(half_type)
    places = (lengths[:, None] - (KCONV - 1) + jnp.arange(KCONV - 1).astype(jnp.int32)[None, :]).astype(jnp.int32)
    conv_tail = x_part[jnp.arange(ROWS).astype(jnp.int32)[:, None], places]
    embedded = embedding[token_ids].astype(float_type)
    normed = normalize(embedded).reshape(DEC * ROWS, D)
    weights_in = dec_in_weight.reshape(2, D, E)
    dec_x = jnp.dot(normed, weights_in[0], preferred_element_type=float_type).astype(half_type).reshape(DEC, ROWS, E)
    dec_z = jnp.dot(normed, weights_in[1], preferred_element_type=float_type).astype(half_type).reshape(DEC, ROWS, E)
    window = jnp.concatenate([jnp.moveaxis(conv_tail, 1, 0), dec_x], axis=0)
    conv_sum = conv_bias.astype(float_type)
    for tap_index in range(KCONV):
        conv_sum = conv_sum + conv_weight[tap_index].astype(float_type) * window[tap_index:tap_index + DEC].astype(float_type)
    dec_conv = jax.nn.silu(conv_sum).astype(half_type)
    dec_flat = dec_conv.reshape(DEC * ROWS, E)
    dec_low = jnp.dot(dec_flat, dt_in_weight, preferred_element_type=float_type)
    dec_bc = jnp.dot(dec_flat, bc_weight, preferred_element_type=float_type).reshape(DEC, ROWS, 2 * NST)
    dec_b = rms_scale(dec_bc[:, :, :NST])
    dec_c = rms_scale(dec_bc[:, :, NST:])
    dec_step = jax.nn.softplus(jnp.dot(normalize(dec_low), dt_proj, preferred_element_type=float_type) + dt_bias).reshape(DEC, ROWS, E)
    conv_float = dec_conv.astype(float_type)
    ssm_state = final_state
    gated_out = []
    for token_step in range(DEC):
        ssm_state, ssm_y = advance_state(decay_rate, ssm_state, (dec_step[token_step], conv_float[token_step], dec_b[token_step], dec_c[token_step]))
        gated_out.append(((ssm_y + d_skip * conv_float[token_step]) * jax.nn.silu(dec_z[token_step].astype(float_type))).astype(half_type))
    gated_flat = jnp.stack(gated_out).reshape(DEC * ROWS, E)
    decoded = jnp.dot(gated_flat, out_weight.reshape(E, D), preferred_element_type=float_type).astype(half_type).reshape(DEC, ROWS, D)
    return (mixed_out, decoded)
```

```python
from functools import partial

import jax
import jax.numpy as jnp
from jax import lax
from jax.experimental import pallas as pl
from jax.experimental.pallas import tpu as pltpu
from jax.sharding import PartitionSpec as P

EPSILON = 1e-06
LOG2E = 1.4426950408889634
MESH = pl.DeviceIdType.MESH
F32 = jnp.float32
BF16 = jnp.bfloat16
SEQ = 32
TP = 4
ROWS = 4
TOK = 128
CH = 2048
NST = 16
ANY = pl.BlockSpec(memory_space=pl.ANY)
VM = pl.BlockSpec(memory_space=pltpu.VMEM)
SM = pl.BlockSpec(memory_space=pltpu.SMEM)
VLIM = 60 * 1024 * 1024


def rms(values, axis):
    return values * lax.rsqrt(jnp.mean(values * values, axis=axis, keepdims=True) + EPSILON)


def silu(values):
    return values * jax.nn.sigmoid(values)


def softplus(values):
    return jnp.maximum(values, 0.0) + jnp.log1p(jnp.exp(-jnp.abs(values)))


def remote(src, dst, send, recv, seq, tp):
    return pltpu.make_async_remote_copy(
        src_ref=src, dst_ref=dst, send_sem=send, recv_sem=recv,
        device_id=(seq, tp), device_id_type=MESH,
    )


def greet_all(seq, tp, with_tp):
    barrier = pltpu.get_barrier_semaphore()

    def one(d, c):
        pl.semaphore_signal(
            barrier, inc=1, device_id=(lax.rem(seq + d, SEQ), tp), device_id_type=MESH
        )
        return c

    lax.fori_loop(1, SEQ, one, 0)
    count = SEQ - 1
    if with_tp:
        for e in range(1, TP):
            pl.semaphore_signal(
                barrier, inc=1, device_id=(seq, lax.rem(tp + e, TP)), device_id_type=MESH
            )
        count += TP - 1
    return barrier, count


def front_kernel(
    len_ref, cw_ref, cb_ref, e_ref, x_hbm, wl_hbm, wb_hbm,
    xc_ref, dn_ref, bc_ref, emb_ref, tail_ref,
    x_v, wl_v, wb_v, halo, xp, low, bct, rlow, rbct, slow, sbct, ssend, sbsend, srecv, sbrecv,
    tsend, trecv, tsum, ebuf, erecv, e2,
    lsem, hsem, tsem, tsem2, t_s, t_r, a_s, a_r, b_s, b_r, c_s, c_r, u_s, u_r,
):
    seq = lax.axis_index("seq")
    tp = lax.axis_index("tp")
    core = lax.rem(tp, 2)
    mate = tp + 1 - 2 * core
    across = lax.rem(tp + 2, TP)
    base = pl.multiple_of(tp * CH, CH)
    loads = [
        pltpu.make_async_copy(x_hbm, x_v, lsem.at[0]),
        pltpu.make_async_copy(wl_hbm.at[pl.ds(base, CH), :], wl_v, lsem.at[1]),
        pltpu.make_async_copy(wb_hbm.at[:, pl.ds(base, CH)], wb_v, lsem.at[2]),
    ]
    for cp in loads:
        cp.start()
    barrier, count = greet_all(seq, tp, True)
    pl.semaphore_wait(barrier, count)
    hcopy = remote(
        x_hbm.at[:, pl.ds(TOK - 16, 16), :], halo, hsem.at[0], hsem.at[1],
        lax.rem(seq + 1, SEQ), tp,
    )
    hcopy.start()
    ea = []
    for e in range(1, TP):
        peer = lax.rem(tp + e, TP)
        cp = remote(e_ref.at[peer], erecv.at[e], a_s.at[e], a_r.at[e], seq, peer)
        cp.start()
        ea.append(cp)
    loads[0].wait()
    pos = seq * TOK + lax.broadcasted_iota(jnp.int32, (16, TOK), 1)
    row = lax.broadcasted_iota(jnp.int32, (16, TOK), 0)
    tail = jnp.zeros((16, CH), F32)
    for r in range(ROWS):
        hit = (row == pos - len_ref[r] + 3 + 4 * r) & (row >= 4 * r) & (row < 4 * r + 3)
        pick = jnp.where(hit, 1.0, 0.0).astype(BF16)
        tail = tail + jnp.dot(pick, x_v[r], preferred_element_type=F32)
    tail = tail.astype(BF16)
    for s in range(16):
        tsend[s] = tail[:, s * 128 : (s + 1) * 128]

    def send_tail(d, c):
        peer = lax.rem(seq + d, SEQ)
        remote(tsend.at[peer // 2], trecv.at[d], t_s.at[d], t_r.at[d], peer, tp).start()
        return c

    lax.fori_loop(1, SEQ, send_tail, 0)
    for cp in ea:
        cp.wait()
    ebuf[...] = (
        (e_ref[tp].astype(F32) + erecv[1].astype(F32))
        + (erecv[2].astype(F32) + erecv[3].astype(F32))
    ).astype(BF16)

    def send_piece(d, c):
        peer = lax.rem(seq + d, SEQ)
        remote(ebuf.at[peer], e2.at[d], b_s.at[d], b_r.at[d], peer, tp).start()
        return c

    lax.fori_loop(1, SEQ, send_piece, 0)
    hcopy.wait()
    keep = jnp.where(seq > 0, 1.0, 0.0).astype(F32)

    def conv_row(r, c):
        for chunk in range(4):
            lanes = pl.ds(chunk * 512, 512)
            wide = pl.ds(pl.multiple_of(base + chunk * 512, 512), 512)
            xp[0:16, :] = halo[r, :, lanes].astype(F32) * keep
            xp[16 : 16 + TOK, :] = x_v[r, :, lanes].astype(F32)
            w = cw_ref[:, wide].astype(F32)
            acc = cb_ref[:, wide].astype(F32) + w[0:1] * xp[13 : 13 + TOK, :]
            for k in range(1, 4):
                acc = acc + w[k : k + 1] * xp[13 + k : 13 + k + TOK, :]
            xc_ref[r, :, lanes] = silu(acc).astype(BF16)
        return c

    lax.fori_loop(0, ROWS, conv_row, 0)
    loads[1].wait()
    loads[2].wait()

    def project(r, c):
        xr = xc_ref[r]
        low[r] = jnp.dot(xr, wl_v[...], preferred_element_type=F32)
        bct[r] = lax.dot_general(
            wb_v[...], xr, (((1,), (1,)), ((), ())), preferred_element_type=F32
        )
        return c

    lax.fori_loop(0, ROWS, project, 0)
    mine = 2 * core
    theirs = 2 - mine
    first = [
        remote(low.at[pl.ds(theirs, 2)], rlow, tsem.at[0], tsem.at[1], seq, mate),
        remote(bct.at[pl.ds(theirs, 2)], rbct, tsem.at[2], tsem.at[3], seq, mate),
    ]
    for cp in first:
        cp.start()

    def wait_tail(d, c):
        peer = lax.rem(seq + SEQ - d, SEQ)
        remote(tsend.at[0], trecv.at[d], t_s.at[d], t_r.at[d], peer, tp).wait()
        return c

    lax.fori_loop(1, SEQ, wait_tail, 0)
    trecv[0] = tsend[seq // 2]
    tsum[...] = jnp.sum(trecv[...].astype(F32), axis=0).astype(BF16)
    tail_ref[tp] = tsum[...]
    tcopies = []
    for e in range(1, TP):
        peer = lax.rem(tp + e, TP)
        cp = remote(tsum, tail_ref.at[tp], u_s.at[e], u_r.at[e], seq, peer)
        cp.start()
        tcopies.append(cp)

    for cp in first:
        cp.wait()
    s_low = low[pl.ds(mine, 2)] + rlow[...]
    s_bct = bct[pl.ds(mine, 2)] + rbct[...]
    slow[...] = s_low
    sbct[...] = s_bct
    ssend[...] = s_low.astype(BF16)
    sbsend[...] = s_bct.astype(BF16)
    second = [
        remote(ssend, srecv, tsem.at[4], tsem.at[5], seq, across),
        remote(sbsend, sbrecv, tsem.at[6], tsem.at[7], seq, across),
    ]
    for cp in second:
        cp.start()

    def wait_piece(d, c):
        peer = lax.rem(seq + SEQ - d, SEQ)
        remote(ebuf.at[0], e2.at[d], b_s.at[d], b_r.at[d], peer, tp).wait()
        return c

    lax.fori_loop(1, SEQ, wait_piece, 0)
    e2[0] = ebuf[seq]
    emb_ref[seq] = jnp.sum(e2[...].astype(F32), axis=0).astype(BF16)

    def send_sum(d, c):
        peer = lax.rem(seq + d, SEQ)
        remote(emb_ref.at[seq], emb_ref.at[seq], c_s.at[d], c_r.at[d], peer, tp).start()
        return c

    lax.fori_loop(1, SEQ, send_sum, 0)

    for cp in second:
        cp.wait()
    t_low = slow[...] + srecv[...].astype(F32)
    t_bct = sbct[...] + sbrecv[...].astype(F32)
    dn_ref[pl.ds(mine, 2)] = rms(t_low, -1).astype(BF16)
    bc_ref[pl.ds(mine, 2)] = jnp.concatenate(
        [rms(t_bct[:, :NST], 1), rms(t_bct[:, NST:], 1)], axis=1
    )
    third = [
        remote(
            dn_ref.at[pl.ds(mine, 2)], dn_ref.at[pl.ds(mine, 2)], tsem2.at[0], tsem2.at[1], seq, mate
        ),
        remote(
            bc_ref.at[pl.ds(mine, 2)], bc_ref.at[pl.ds(mine, 2)], tsem2.at[2], tsem2.at[3], seq, mate
        ),
    ]
    for cp in third:
        cp.start()
    for cp in third:
        cp.wait()
    for cp in tcopies:
        cp.wait()

    def wait_sum(d, c):
        peer = lax.rem(seq + SEQ - d, SEQ)
        remote(emb_ref.at[seq], emb_ref.at[peer], c_s.at[d], c_r.at[d], peer, tp).wait()
        return c

    lax.fori_loop(1, SEQ, wait_sum, 0)


def front(lengths, conv_weight, conv_bias, e_terms, x_part, dt_in_weight, bc_weight_t):
    dma = pltpu.SemaphoreType.DMA
    return pl.pallas_call(
        front_kernel,
        out_shape=(
            jax.ShapeDtypeStruct((ROWS, TOK, CH), BF16),
            jax.ShapeDtypeStruct((ROWS, TOK, 256), BF16),
            jax.ShapeDtypeStruct((ROWS, 32, TOK), F32),
            jax.ShapeDtypeStruct((SEQ, 8, 128), BF16),
            jax.ShapeDtypeStruct((TP, 16, 128), BF16),
        ),
        in_specs=[SM, VM, VM, VM, ANY, ANY, ANY],
        out_specs=(VM,) * 5,
        scratch_shapes=[
            pltpu.VMEM((ROWS, TOK, CH), BF16),
            pltpu.VMEM((CH, 256), BF16),
            pltpu.VMEM((32, CH), BF16),
            pltpu.VMEM((ROWS, 16, CH), BF16),
            pltpu.VMEM((16 + TOK, 512), F32),
            pltpu.VMEM((ROWS, TOK, 256), F32),
            pltpu.VMEM((ROWS, 32, TOK), F32),
            pltpu.VMEM((2, TOK, 256), F32),
            pltpu.VMEM((2, 32, TOK), F32),
            pltpu.VMEM((2, TOK, 256), F32),
            pltpu.VMEM((2, 32, TOK), F32),
            pltpu.VMEM((2, TOK, 256), BF16),
            pltpu.VMEM((2, 32, TOK), BF16),
            pltpu.VMEM((2, TOK, 256), BF16),
            pltpu.VMEM((2, 32, TOK), BF16),
            pltpu.VMEM((16, 16, 128), BF16),
            pltpu.VMEM((SEQ, 16, 128), BF16),
            pltpu.VMEM((16, 128), BF16),
            pltpu.VMEM((SEQ, 8, 128), BF16),
            pltpu.VMEM((TP, SEQ, 8, 128), BF16),
            pltpu.VMEM((SEQ, 8, 128), BF16),
            dma((3,)), dma((2,)), dma((8,)), dma((4,)),
            dma((SEQ,)), dma((SEQ,)), dma((TP,)), dma((TP,)), dma((SEQ,)), dma((SEQ,)),
            dma((SEQ,)), dma((SEQ,)), dma((TP,)), dma((TP,)),
        ],
        compiler_params=pltpu.CompilerParams(
            collective_id=0, has_side_effects=True, vmem_limit_bytes=VLIM
        ),
        name="front",
    )(lengths, conv_weight, conv_bias, e_terms, x_part, dt_in_weight, bc_weight_t)


def spread_columns(bc, bcl_ref, first, count):
    for t in range(TOK):
        col = bc[first : first + count, t : t + 1]
        bcl_ref[t * count : (t + 1) * count, :] = jnp.broadcast_to(col, (count, 128))


def rates_to_scan(a_ref, base, a_s):
    for s in range(16):
        lanes = pl.ds(pl.multiple_of(base + s * 128, 128), 128)
        a_s[pl.ds(s, NST, stride=16), :] = -jnp.exp(a_ref[:, lanes]) * LOG2E


def state_kernel(
    len_ref, dn_ref, xc_ref, bc_ref, bias_ref, a_ref, wp_hbm,
    dt_ref, u_ref, send_ref,
    wp_v, a_s, b_l, sem,
):
    r = pl.program_id(0)
    seq = lax.axis_index("seq")
    base = pl.multiple_of(lax.axis_index("tp") * CH, CH)

    @pl.when(r == 0)
    def _():
        cp = pltpu.make_async_copy(wp_hbm.at[:, pl.ds(base, CH)], wp_v, sem)
        cp.start()
        rates_to_scan(a_ref, base, a_s)
        cp.wait()

    spread_columns(bc_ref[0], b_l, 0, NST)
    pos = seq * TOK + lax.broadcasted_iota(jnp.int32, (TOK, 128), 0)
    valid = jnp.where(pos < len_ref[r], 1.0, 0.0)
    dn = dn_ref[0]
    for s in range(16):
        lanes = pl.ds(s * 128, 128)
        v = jnp.dot(dn, wp_v[:, lanes], preferred_element_type=F32)
        v = v + bias_ref[:, pl.ds(pl.multiple_of(base + s * 128, 128), 128)]
        dt = softplus(v) * valid
        dt_ref[0, pl.ds(s, TOK, stride=16), :] = dt
        u_ref[0, pl.ds(s, TOK, stride=16), :] = dt * xc_ref[0, :, lanes].astype(F32)
    for half in range(2):
        rates = [a_s[n * 16 + half * 8 : n * 16 + half * 8 + 8, :] for n in range(NST)]

        def step(t, carry):
            total, hs = carry[0], carry[1:]
            at = pl.ds(pl.multiple_of(t * 16 + half * 8, 8), 8)
            dt = dt_ref[0, at, :]
            u = u_ref[0, at, :]
            new = []
            for n in range(NST):
                b = b_l[pl.ds(t * NST + n, 8, stride=0), :]
                new.append(jnp.exp2(dt * rates[n]) * hs[n] + u * b)
            return (total + dt, *new)

        zero = jnp.zeros((8, 128), F32)
        out = lax.fori_loop(0, TOK, step, (zero,) * (NST + 1), unroll=2)
        for nh in range(2):
            start = (16 * half + nh) * 40
            send_ref[pl.ds(start + 32 + r, 8, stride=80), :] = out[0]
            for n in range(8):
                send_ref[pl.ds(start + r * 8 + n, 8, stride=80), :] = out[1 + nh * 8 + n]


def states(lengths, dn, xc, bc, dt_bias, a_log, dt_proj):
    row = lambda *shape: pl.BlockSpec((1,) + shape, lambda r: (r,) + (0,) * len(shape))
    whole = lambda *shape: pl.BlockSpec(shape, lambda r: (0,) * len(shape))
    return pl.pallas_call(
        state_kernel,
        grid=(ROWS,),
        out_shape=(
            jax.ShapeDtypeStruct((ROWS, TOK * 16, 128), F32),
            jax.ShapeDtypeStruct((ROWS, TOK * 16, 128), F32),
            jax.ShapeDtypeStruct((SEQ * 40, 128), F32),
        ),
        in_specs=[
            SM, row(TOK, 256), row(TOK, CH), row(32, TOK), whole(1, 8192), whole(16, 8192), ANY,
        ],
        out_specs=(row(TOK * 16, 128), row(TOK * 16, 128), whole(SEQ * 40, 128)),
        scratch_shapes=[
            pltpu.VMEM((256, CH), BF16),
            pltpu.VMEM((256, 128), F32),
            pltpu.VMEM((TOK * NST, 128), F32),
            pltpu.SemaphoreType.DMA,
        ],
        compiler_params=pltpu.CompilerParams(vmem_limit_bytes=VLIM),
        name="states",
    )(lengths, dn, xc, bc, dt_bias, a_log, dt_proj)


def output_kernel(
    len_ref, dt_ref, u_ref, bc_ref, inc_ref, xc_ref, z_ref, skip_ref, a_ref,
    out_ref, a_s, bc_l, y_s,
):
    r = pl.program_id(0)
    seq = lax.axis_index("seq")
    base = pl.multiple_of(lax.axis_index("tp") * CH, CH)

    @pl.when(r == 0)
    def _():
        rates_to_scan(a_ref, base, a_s)

    spread_columns(bc_ref[0], bc_l, 0, 32)
    for half in range(2):
        rates = [a_s[n * 16 + half * 8 : n * 16 + half * 8 + 8, :] for n in range(NST)]

        def step(t, hs):
            at = pl.ds(pl.multiple_of(t * 16 + half * 8, 8), 8)
            dt = dt_ref[0, at, :]
            u = u_ref[0, at, :]
            new = []
            sums = [None] * 4
            for n in range(NST):
                b = bc_l[pl.ds(t * 32 + n, 8, stride=0), :]
                c = bc_l[pl.ds(t * 32 + NST + n, 8, stride=0), :]
                h = jnp.exp2(dt * rates[n]) * hs[n] + u * b
                new.append(h)
                term = h * c
                sums[n % 4] = term if sums[n % 4] is None else sums[n % 4] + term
            y_s[at, :] = (sums[0] + sums[1]) + (sums[2] + sums[3])
            return tuple(new)

        first = []
        for n in range(NST):
            start = (16 * half + n // 8) * 32 + r * 8 + n % 8
            first.append(inc_ref[pl.ds(start, 8, stride=64), :])
        lax.fori_loop(0, TOK, step, tuple(first), unroll=2)
    pos = seq * TOK + lax.broadcasted_iota(jnp.int32, (TOK, 128), 0)
    valid = jnp.where(pos < len_ref[r], 1.0, 0.0)
    for s in range(16):
        lanes = pl.ds(s * 128, 128)
        y = y_s[pl.ds(s, TOK, stride=16), :]
        skip = skip_ref[:, pl.ds(pl.multiple_of(base + s * 128, 128), 128)]
        z = z_ref[0, :, lanes].astype(F32)
        gated = (y + skip * xc_ref[0, :, lanes].astype(F32)) * silu(z) * valid
        out_ref[0, :, lanes] = gated.astype(BF16)


def outputs(lengths, dt, u, bc, incoming, xc, z_part, d_skip, a_log):
    row = lambda *shape: pl.BlockSpec((1,) + shape, lambda r: (r,) + (0,) * len(shape))
    whole = lambda *shape: pl.BlockSpec(shape, lambda r: (0,) * len(shape))
    return pl.pallas_call(
        output_kernel,
        grid=(ROWS,),
        out_shape=jax.ShapeDtypeStruct((ROWS, TOK, CH), BF16),
        in_specs=[
            SM, row(TOK * 16, 128), row(TOK * 16, 128), row(32, TOK), whole(SEQ * 32, 128),
            row(TOK, CH), row(TOK, CH), whole(1, 8192), whole(16, 8192),
        ],
        out_specs=row(TOK, CH),
        scratch_shapes=[
            pltpu.VMEM((256, 128), F32),
            pltpu.VMEM((TOK * 32, 128), F32),
            pltpu.VMEM((TOK * 16, 128), F32),
        ],
        compiler_params=pltpu.CompilerParams(vmem_limit_bytes=VLIM),
        name="outputs",
    )(lengths, dt, u, bc, incoming, xc, z_part, d_skip, a_log)


def carry_kernel(
    send_ref, p_ref, a_hbm,
    inc_ref, fin_ref, pall_ref,
    a_v, recv, ret, final,
    asem, s_s, s_r, r_s, r_r, p_s, p_r, f_s, f_r,
):
    seq = lax.axis_index("seq")
    tp = lax.axis_index("tp")
    part = seq // 2
    nh = lax.rem(seq, 2)
    acopy = pltpu.make_async_copy(
        a_hbm.at[
            pl.ds(pl.multiple_of(nh * 8, 8), 8),
            pl.ds(pl.multiple_of(tp * CH + part * 128, 128), 128),
        ],
        a_v, asem,
    )
    acopy.start()
    barrier, count = greet_all(seq, tp, False)
    for e in range(2):
        for d in range(1, TP):
            pl.semaphore_signal(
                barrier, inc=1,
                device_id=(seq + e * (1 - 2 * nh), lax.rem(tp + d, TP)), device_id_type=MESH,
            )
            count += 1
    pl.semaphore_wait(barrier, count)

    def send_state(d, c):
        peer = lax.rem(seq + d, SEQ)
        remote(send_ref.at[peer], recv.at[seq], s_s.at[d], s_r.at[d], peer, tp).start()
        return c

    lax.fori_loop(1, SEQ, send_state, 0)

    def send_p(d, c):
        peer = lax.rem(seq + d, SEQ)
        remote(p_ref, pall_ref.at[seq], p_s.at[d], p_r.at[d], peer, tp).start()
        return c

    lax.fori_loop(1, SEQ, send_p, 0)
    recv[seq] = send_ref[seq]
    pall_ref[seq] = p_ref[...]
    acopy.wait()
    rate = -jnp.exp(a_v[...]) * LOG2E

    def wait_state(d, c):
        peer = lax.rem(seq + SEQ - d, SEQ)
        remote(send_ref.at[0], recv.at[peer], s_s.at[d], s_r.at[d], peer, tp).wait()
        return c

    lax.fori_loop(1, SEQ, wait_state, 0)

    def combine(q, carry):
        new = []
        for r in range(ROWS):
            ret[q, r * 8 : r * 8 + 8, :] = carry[r]
            total = recv[q, 32 + r : 33 + r, :]
            new.append(jnp.exp2(rate * total) * carry[r] + recv[q, r * 8 : r * 8 + 8, :])
        return tuple(new)

    zero = jnp.zeros((8, 128), F32)
    last = lax.fori_loop(0, SEQ, combine, (zero,) * ROWS)
    for r in range(ROWS):
        final[r] = last[r]

    def send_back(d, c):
        peer = lax.rem(seq + d, SEQ)
        remote(ret.at[peer], inc_ref.at[seq], r_s.at[d], r_r.at[d], peer, tp).start()
        return c

    lax.fori_loop(1, SEQ, send_back, 0)
    slot = tp * 2 + nh
    fcopies = []
    for e in range(2):
        for d in range(TP):
            if e == 0 and d == 0:
                continue
            peer_seq = seq + e * (1 - 2 * nh)
            peer_tp = lax.rem(tp + d, TP)
            cp = remote(
                final.at[peer_tp], fin_ref.at[slot],
                f_s.at[e * TP + d], f_r.at[e * TP + d], peer_seq, peer_tp,
            )
            cp.start()
            fcopies.append((e, d, cp))
    inc_ref[seq] = ret[seq]
    fin_ref[slot] = final[tp]

    def wait_back(d, c):
        peer = lax.rem(seq + SEQ - d, SEQ)
        remote(ret.at[0], inc_ref.at[peer], r_s.at[d], r_r.at[d], peer, tp).wait()
        return c

    lax.fori_loop(1, SEQ, wait_back, 0)

    def wait_p(d, c):
        peer = lax.rem(seq + SEQ - d, SEQ)
        remote(p_ref, pall_ref.at[peer], p_s.at[d], p_r.at[d], peer, tp).wait()
        return c

    lax.fori_loop(1, SEQ, wait_p, 0)
    for e, d, cp in fcopies:
        cp.wait()


def carries(send, p, a_log):
    dma = pltpu.SemaphoreType.DMA
    return pl.pallas_call(
        carry_kernel,
        out_shape=(
            jax.ShapeDtypeStruct((SEQ, 32, 128), F32),
            jax.ShapeDtypeStruct((8, 8, 128), F32),
            jax.ShapeDtypeStruct((SEQ, 16, 128), BF16),
        ),
        in_specs=[VM, VM, ANY],
        out_specs=(VM,) * 3,
        scratch_shapes=[
            pltpu.VMEM((8, 128), F32),
            pltpu.VMEM((SEQ, 40, 128), F32),
            pltpu.VMEM((SEQ, 32, 128), F32),
            pltpu.VMEM((ROWS, 8, 128), F32),
            dma, dma((SEQ,)), dma((SEQ,)), dma((SEQ,)), dma((SEQ,)), dma((SEQ,)), dma((SEQ,)),
            dma((8,)), dma((8,)),
        ],
        compiler_params=pltpu.CompilerParams(
            collective_id=1, has_side_effects=True, vmem_limit_bytes=VLIM
        ),
        name="carries",
    )(send, p, a_log)


def token_kernel(
    emb_ref, tail_ref, cw_ref, cb_ref, wt_hbm, wl_hbm, wb_hbm,
    p_ref, dc_ref, dz_ref,
    wt_v, wl_v, wb_v, nb, win, pk, sem,
):
    seq = lax.axis_index("seq")
    tp = lax.axis_index("tp")
    part = seq // 2
    copies = [pltpu.make_async_copy(wt_hbm, wt_v, sem.at[0])]
    for g in range(TP):
        at = pl.ds(pl.multiple_of(g * CH + part * 128, 128), 128)
        copies.append(pltpu.make_async_copy(wl_hbm.at[at, :], wl_v.at[g], sem.at[1 + g]))
        copies.append(pltpu.make_async_copy(wb_hbm.at[:, at], wb_v.at[g], sem.at[5 + g]))
    for cp in copies:
        cp.start()
    square = jnp.zeros((8, 128), F32)
    for p in range(SEQ):
        v = emb_ref[p].astype(F32)
        square = square + v * v
    scale = lax.rsqrt(jnp.sum(square, axis=1, keepdims=True) / 4096.0 + EPSILON)
    for p in range(SEQ):
        nb[:, p * 128 : (p + 1) * 128] = (emb_ref[p].astype(F32) * scale).astype(BF16)
    for cp in copies:
        cp.wait()
    both = lax.dot_general(
        nb[...], wt_v[...], (((1,), (1,)), ((), ())), preferred_element_type=F32
    )
    both = both.astype(BF16).astype(F32)
    lane = lax.broadcasted_iota(jnp.int32, (8, 128), 1)
    sub = lax.broadcasted_iota(jnp.int32, (8, 128), 0)
    own = (lane // 64 == lax.rem(seq, 2)) & (sub < 3)
    low = jnp.zeros((8, 256), F32)
    bc = jnp.zeros((8, 32), F32)
    for g in range(TP):
        at = pl.ds(pl.multiple_of(g * CH + part * 128, 128), 128)
        x = both[:, g * 64 : g * 64 + 64]
        z = both[:, 256 + g * 64 : 256 + g * 64 + 64]
        t = tail_ref[g].astype(F32)
        head = jnp.zeros((4, 128), F32)
        for k in range(TP):
            head = head + jnp.where(tp == k, t[k * 4 : k * 4 + 4], 0.0)
        win[0:4, :] = head
        win[3:11, :] = jnp.concatenate([x, x], axis=1)
        w = cw_ref[:, at].astype(F32)
        acc = cb_ref[:, at].astype(F32)
        for k in range(4):
            acc = acc + w[k : k + 1] * win[k : k + 8, :]
        conv = jnp.where(own, silu(acc), 0.0).astype(BF16)
        low = low + jnp.dot(conv, wl_v[g], preferred_element_type=F32)
        bc = bc + lax.dot_general(
            conv, wb_v[g], (((1,), (1,)), ((), ())), preferred_element_type=F32
        )
        dc_ref[g] = conv.astype(F32)
        dz_ref[g] = jnp.concatenate([z, z], axis=1)
    pk[...] = jnp.zeros((16, 128), F32)
    pk[0:4, :] = low[0:4, 0:128]
    pk[4:8, :] = low[0:4, 128:256]
    pk[8:12, 0:32] = bc[0:4]
    p_ref[...] = pk[...].astype(BF16)


def tokens(emb, tail, conv_weight, conv_bias, w_t, dt_in_weight, bc_weight_t):
    return pl.pallas_call(
        token_kernel,
        out_shape=(
            jax.ShapeDtypeStruct((16, 128), BF16),
            jax.ShapeDtypeStruct((TP, 8, 128), F32),
            jax.ShapeDtypeStruct((TP, 8, 128), F32),
        ),
        in_specs=[VM, VM, VM, VM, ANY, ANY, ANY],
        out_specs=(VM,) * 3,
        scratch_shapes=[
            pltpu.VMEM((512, 4096), BF16),
            pltpu.VMEM((TP, 128, 256), BF16),
            pltpu.VMEM((TP, 32, 128), BF16),
            pltpu.VMEM((8, 4096), BF16),
            pltpu.VMEM((16, 128), F32),
            pltpu.VMEM((16, 128), F32),
            pltpu.SemaphoreType.DMA((9,)),
        ],
        compiler_params=pltpu.CompilerParams(vmem_limit_bytes=VLIM),
        name="tokens",
    )(emb, tail, conv_weight, conv_bias, w_t, dt_in_weight, bc_weight_t)


def decode_kernel(
    pall_ref, fin_ref, dc_ref, dz_ref, bias_ref, skip_ref, a_hbm, wp_hbm, ow_hbm,
    out_ref,
    a_v, wp_v, ow_v, pk, obuf, orecv, osum, fo,
    sem, s_s, s_r, b_s, b_r,
):
    seq = lax.axis_index("seq")
    tp = lax.axis_index("tp")
    part = seq // 2
    copies = [pltpu.make_async_copy(ow_hbm, ow_v, sem.at[0])]
    for g in range(TP):
        at = pl.ds(pl.multiple_of(g * CH + part * 128, 128), 128)
        copies.append(pltpu.make_async_copy(wp_hbm.at[:, at], wp_v.at[g], sem.at[1 + g]))
        copies.append(pltpu.make_async_copy(a_hbm.at[:, at], a_v.at[g], sem.at[5 + g]))
    for cp in copies:
        cp.start()
    barrier, count = greet_all(seq, tp, False)
    pk[0:16, :] = jnp.sum(pall_ref[...].astype(F32), axis=0)
    lo = pk[0:8, :]
    hi = pk[4:12, :]
    bc = pk[8:16, :]
    norm = lax.rsqrt(
        (jnp.sum(lo * lo, axis=1, keepdims=True) + jnp.sum(hi * hi, axis=1, keepdims=True)) / 256.0
        + EPSILON
    )
    lane = lax.broadcasted_iota(jnp.int32, (8, 128), 1)
    squares = bc * bc
    b_ms = jnp.sum(jnp.where(lane < NST, squares, 0.0), axis=1, keepdims=True) / NST
    c_ms = (
        jnp.sum(jnp.where((lane >= NST) & (lane < 2 * NST), squares, 0.0), axis=1, keepdims=True)
        / NST
    )
    bc = bc * jnp.where(lane < NST, lax.rsqrt(b_ms + EPSILON), lax.rsqrt(c_ms + EPSILON))
    bct = jnp.transpose(bc)
    lo = (lo * norm).astype(BF16)
    hi = (hi * norm).astype(BF16)
    for cp in copies:
        cp.wait()
    half = lax.rem(seq, 2)
    total = jnp.zeros((8, 4096), F32)
    sub = lax.broadcasted_iota(jnp.int32, (8, 128), 0)
    for g in range(TP):
        at = pl.ds(pl.multiple_of(g * CH + part * 128, 128), 128)
        v = jnp.dot(lo, wp_v[g, 0:128, :], preferred_element_type=F32)
        v = v + jnp.dot(hi, wp_v[g, 128:256, :], preferred_element_type=F32)
        dt = softplus(v + bias_ref[:, at])
        x = dc_ref[g]
        u = dt * x
        y = jnp.zeros((8, 128), F32)
        for nh in range(2):
            rate = -jnp.exp(a_v[g, nh * 8 : nh * 8 + 8, :]) * LOG2E
            st = fin_ref[g * 2 + nh]
            for j in range(3):
                b = jnp.broadcast_to(bct[nh * 8 : nh * 8 + 8, j : j + 1], (8, 128))
                c = jnp.broadcast_to(bct[NST + nh * 8 : NST + nh * 8 + 8, j : j + 1], (8, 128))
                st = jnp.exp2(rate * dt[j : j + 1]) * st + u[j : j + 1] * b
                y = y + jnp.where(sub == j, jnp.sum(st * c, axis=0, keepdims=True), 0.0)
        z = dz_ref[g]
        gated = ((y + skip_ref[:, at] * x) * silu(z)).astype(BF16).astype(F32)
        mine = jnp.where(half == 1, gated[:, 64:128], gated[:, 0:64]).astype(BF16)
        total = total + jnp.dot(mine, ow_v[g], preferred_element_type=F32)
    for p in range(SEQ):
        obuf[p] = total[:, p * 128 : (p + 1) * 128]
    pl.semaphore_wait(barrier, count)

    def send_part(d, c):
        peer = lax.rem(seq + d, SEQ)
        remote(obuf.at[peer], orecv.at[d], s_s.at[d], s_r.at[d], peer, tp).start()
        return c

    lax.fori_loop(1, SEQ, send_part, 0)
    orecv[0] = obuf[seq]

    def wait_part(d, c):
        peer = lax.rem(seq + SEQ - d, SEQ)
        remote(obuf.at[0], orecv.at[d], s_s.at[d], s_r.at[d], peer, tp).wait()
        return c

    lax.fori_loop(1, SEQ, wait_part, 0)
    osum[...] = jnp.sum(orecv[...], axis=0).astype(BF16)

    def send_sum(d, c):
        peer = lax.rem(seq + d, SEQ)
        remote(osum, fo.at[seq], b_s.at[d], b_r.at[d], peer, tp).start()
        return c

    lax.fori_loop(1, SEQ, send_sum, 0)
    fo[seq] = osum[...]

    def wait_sum(d, c):
        peer = lax.rem(seq + SEQ - d, SEQ)
        remote(osum, fo.at[peer], b_s.at[d], b_r.at[d], peer, tp).wait()
        return c

    lax.fori_loop(1, SEQ, wait_sum, 0)
    for p in range(SEQ):
        out_ref[:, p * 128 : (p + 1) * 128] = fo[p].astype(F32)[0:3].astype(BF16)


def decode(pall, fin, dc, dz, dt_bias, d_skip, a_log, dt_proj, out_weight):
    dma = pltpu.SemaphoreType.DMA
    return pl.pallas_call(
        decode_kernel,
        out_shape=jax.ShapeDtypeStruct((3, 4096), BF16),
        in_specs=[VM, VM, VM, VM, VM, VM, ANY, ANY, ANY],
        out_specs=VM,
        scratch_shapes=[
            pltpu.VMEM((TP, NST, 128), F32),
            pltpu.VMEM((TP, 256, 128), BF16),
            pltpu.VMEM((TP, 64, 4096), BF16),
            pltpu.VMEM((16, 128), F32),
            pltpu.VMEM((SEQ, 8, 128), F32),
            pltpu.VMEM((SEQ, 8, 128), F32),
            pltpu.VMEM((8, 128), BF16),
            pltpu.VMEM((SEQ, 8, 128), BF16),
            dma((9,)), dma((SEQ,)), dma((SEQ,)), dma((SEQ,)), dma((SEQ,)),
        ],
        compiler_params=pltpu.CompilerParams(
            collective_id=2, has_side_effects=True, vmem_limit_bytes=VLIM
        ),
        name="decode",
    )(pall, fin, dc, dz, dt_bias, d_skip, a_log, dt_proj, out_weight)


def shards(
    x_part, z_part, conv_weight, conv_bias, dt_in_weight, bc_weight, dt_proj, dt_bias, a_log,
    d_skip, lengths, token_ids, embedding, dec_in_weight, out_weight,
):
    seq_pos = lax.axis_index("seq")
    tp_pos = lax.axis_index("tp")
    vocab = embedding.shape[0]
    ids = token_ids - (seq_pos * TP + tp_pos) * vocab
    ids = jnp.pad(ids, ((0, 5), (0, 0)), constant_values=-1).T.reshape(32)
    hot = (ids[:, None] == jnp.arange(vocab, dtype=jnp.int32)[None, :]).astype(BF16)
    e_terms = jnp.dot(hot, embedding, preferred_element_type=F32).astype(BF16)
    e_terms = e_terms.reshape(ROWS, 8, SEQ, 128).transpose(0, 2, 1, 3)
    cb = conv_bias.reshape(1, -1)
    bias = dt_bias.reshape(1, -1)
    skip = d_skip.reshape(1, -1)
    bc_t = bc_weight.T
    w_t = jnp.transpose(dec_in_weight, (0, 2, 3, 1)).reshape(512, 4096)
    xc, dn, bc, emb, tail = front(
        lengths, conv_weight, cb, e_terms, x_part, dt_in_weight, bc_t
    )
    p, dc, dz = tokens(emb, tail, conv_weight, cb, w_t, dt_in_weight, bc_t)
    dt, u, send = states(lengths, dn, xc, bc, bias, a_log, dt_proj)
    inc, fin, pall = carries(send.reshape(SEQ, 40, 128), p, a_log)
    mixed_out = outputs(lengths, dt, u, bc, inc.reshape(SEQ * 32, 128), xc, z_part, skip, a_log)
    decoded = decode(pall, fin, dc, dz, bias, skip, a_log, dt_proj, out_weight)
    return (mixed_out, decoded.reshape(3, 1, 4096))


def solution(mesh):
    return jax.shard_map(
        shards,
        mesh=mesh,
        in_specs=(
            P(None, "seq", "tp"), P(None, "seq", "tp"), P(), P(), P(), P(), P(), P(), P(), P(),
            P(), P(), P(("seq", "tp"), None), P(None, None, None, "seq"), P(None, "seq", None),
        ),
        out_specs=(P(None, "seq", "tp"), P(None, "tp", None)),
        check_vma=False,
    )
```

```python
from functools import partial

import jax
import jax.numpy as jnp
from jax import lax
from jax.experimental import pallas as pl
from jax.experimental.pallas import tpu as pltpu
from jax.sharding import PartitionSpec as P

EPSILON = 1e-06
LOG2E = 1.4426950408889634
MESH = pl.DeviceIdType.MESH
F32 = jnp.float32
BF16 = jnp.bfloat16
SEQ = 32
TP = 4
ROWS = 4
TOK = 128
CH = 2048
NST = 16
ANY = pl.BlockSpec(memory_space=pl.ANY)
VM = pl.BlockSpec(memory_space=pltpu.VMEM)
SM = pl.BlockSpec(memory_space=pltpu.SMEM)
VLIM = 60 * 1024 * 1024


def rms(values, axis):
    return values * lax.rsqrt(jnp.mean(values * values, axis=axis, keepdims=True) + EPSILON)


def silu(values):
    return values * jax.nn.sigmoid(values)


def softplus(values):
    return jnp.maximum(values, 0.0) + jnp.log1p(jnp.exp(-jnp.abs(values)))


def remote(src, dst, send, recv, seq, tp):
    return pltpu.make_async_remote_copy(
        src_ref=src, dst_ref=dst, send_sem=send, recv_sem=recv,
        device_id=(seq, tp), device_id_type=MESH,
    )

PITCH = 136


def for_peers(seq, fn):
    def one(d, c):
        fn(d, lax.rem(seq + d, SEQ))
        return c

    lax.fori_loop(1, SEQ, one, 0)


class Refs:
    pass


def lanes_at(g, part):
    return pl.ds(pl.multiple_of(g * CH + part * 128, 128), 128)


def token_terms(k, seq, tp):
    row = lax.broadcasted_iota(jnp.int32, (32, 512), 0)
    ids = jnp.full((32, 512), -1, jnp.int32)
    for j in range(3):
        for r in range(ROWS):
            ids = jnp.where(row == r * 8 + j, k.ids[j, r], ids)
    here = (seq * TP + tp) * 512 + lax.broadcasted_iota(jnp.int32, (32, 512), 1)
    hot = jnp.where(ids == here, 1.0, 0.0).astype(BF16)
    k.emb_load.wait()
    for p in range(0, SEQ, 4):
        res = jnp.dot(hot, k.emb_v[:, p * 128 : p * 128 + 512], preferred_element_type=F32)
        for r in range(ROWS):
            for i in range(4):
                k.e_s[r, p + i] = res[r * 8 : r * 8 + 8, i * 128 : i * 128 + 128].astype(BF16)


def tail_terms(k, seq):
    pos = seq * TOK + lax.broadcasted_iota(jnp.int32, (16, TOK), 1)
    row = lax.broadcasted_iota(jnp.int32, (16, TOK), 0)
    picks = []
    for r in range(ROWS):
        hit = (row == pos - k.len[r] + 3 + 4 * r) & (row >= 4 * r) & (row < 4 * r + 3)
        picks.append(jnp.where(hit, 1.0, 0.0).astype(BF16))
    for s in range(0, 16, 4):
        lanes = pl.ds(s * 128, 512)
        tail = jnp.dot(picks[0], k.x_v[0, :, lanes], preferred_element_type=F32)
        for r in range(1, ROWS):
            tail = tail + jnp.dot(picks[r], k.x_v[r, :, lanes], preferred_element_type=F32)
        tail = tail.astype(BF16)
        for i in range(4):
            k.tsend[s + i] = tail[:, i * 128 : i * 128 + 128]


def conv_project(k, r, base, keep):
    def chunk(ch, c):
        lanes = pl.ds(pl.multiple_of(ch * 512, 512), 512)
        wide = pl.ds(pl.multiple_of(base + ch * 512, 512), 512)
        k.xp[0:16, :] = k.halo[r, :, lanes].astype(F32) * keep
        k.xp[16 : 16 + TOK, :] = k.x_v[r, :, lanes].astype(F32)
        w = k.cw[:, wide].astype(F32)
        acc = k.cb[:, wide].astype(F32) + w[0:1] * k.xp[13 : 13 + TOK, :]
        for tap in range(1, 4):
            acc = acc + w[tap : tap + 1] * k.xp[13 + tap : 13 + tap + TOK, :]
        k.xc[r, :, lanes] = silu(acc).astype(BF16)
        return c

    lax.fori_loop(0, 4, chunk, 0)
    xr = k.xc[r]
    k.low[r, 0:TOK, :] = jnp.dot(xr, k.wl_v[...], preferred_element_type=F32)
    bct = lax.dot_general(k.wb_v[...], xr, (((1,), (1,)), ((), ())), preferred_element_type=F32)
    k.low[r, TOK : TOK + 16, 0:128] = bct[0:NST]
    k.low[r, TOK : TOK + 16, 128:256] = bct[NST:]


def spread_columns(k, r):
    bc = k.bc[r]
    for t in range(TOK):
        k.bcl[r, t * 32 : t * 32 + 32, :] = jnp.broadcast_to(bc[:, t : t + 1], (32, 128))


def step_sizes(k, r, seq, base):
    pos = seq * TOK + lax.broadcasted_iota(jnp.int32, (TOK, 128), 0)
    valid = jnp.where(pos < k.len[r], 1.0, 0.0)
    dn = k.dn[r]
    for s in range(0, 16, 2):
        v2 = jnp.dot(dn, k.wp_v[:, s * 128 : s * 128 + 256], preferred_element_type=F32)
        for i in range(2):
            lanes = pl.ds((s + i) * 128, 128)
            v = v2[:, i * 128 : i * 128 + 128]
            v = v + k.bias[:, pl.ds(pl.multiple_of(base + (s + i) * 128, 128), 128)]
            dt = softplus(v) * valid
            k.dt[r, (s + i) * PITCH : (s + i) * PITCH + TOK, :] = dt
            k.u[r, (s + i) * PITCH : (s + i) * PITCH + TOK, :] = dt * k.xc[r, :, lanes].astype(F32)


def pass_one(k, r, pair, i):
    for half in range(2):
        rates = [k.a_s[n * 16 + half * 8 : n * 16 + half * 8 + 8, :] for n in range(NST)]

        def step(t, carry):
            at = pl.ds(half * 8 * PITCH + t, 8, stride=PITCH)
            dt = k.dt[r, at, :]
            u = k.u[r, at, :]
            new = [carry[0] + dt]
            for n in range(NST):
                b = k.bcl[r, pl.ds(t * 32 + n, 8, stride=0), :]
                new.append(jnp.exp2(dt * rates[n]) * carry[n + 1] + u * b)
            return tuple(new)

        zero = jnp.zeros((8, 128), F32)
        out = lax.fori_loop(0, TOK, step, (zero,) * (NST + 1), unroll=4)
        for nh in range(2):
            start = (nh * 16 + half * 8) * 24
            k.send[pair, pl.ds(start + 16 + i, 8, stride=24), :] = out[0]
            for n in range(8):
                k.send[pair, pl.ds(start + i * 8 + n, 8, stride=24), :] = out[1 + nh * 8 + n]


def pass_two(k, r, pair, i, seq, base):
    for half in range(2):
        rates = [k.a_s[n * 16 + half * 8 : n * 16 + half * 8 + 8, :] for n in range(NST)]

        def step(t, hs):
            at = pl.ds(half * 8 * PITCH + t, 8, stride=PITCH)
            dt = k.dt[r, at, :]
            u = k.u[r, at, :]
            new = []
            sums = [None] * 4
            for n in range(NST):
                b = k.bcl[r, pl.ds(t * 32 + n, 8, stride=0), :]
                c = k.bcl[r, pl.ds(t * 32 + NST + n, 8, stride=0), :]
                h = jnp.exp2(dt * rates[n]) * hs[n] + u * b
                new.append(h)
                term = h * c
                sums[n % 4] = term if sums[n % 4] is None else sums[n % 4] + term
            k.y_s[at, :] = (sums[0] + sums[1]) + (sums[2] + sums[3])
            return tuple(new)

        first = []
        for n in range(NST):
            start = (n // 8 * 16 + half * 8) * 24 + i * 8 + n % 8
            first.append(k.inc[pair, pl.ds(start, 8, stride=24), :])
        lax.fori_loop(0, TOK, step, tuple(first), unroll=4)
    pos = seq * TOK + lax.broadcasted_iota(jnp.int32, (TOK, 128), 0)
    valid = jnp.where(pos < k.len[r], 1.0, 0.0)
    for s in range(16):
        lanes = pl.ds(s * 128, 128)
        y = k.y_s[s * PITCH : s * PITCH + TOK, :]
        skip = k.skip[:, pl.ds(pl.multiple_of(base + s * 128, 128), 128)]
        z = k.z_v[r, :, lanes].astype(F32)
        gated = (y + skip * k.xc[r, :, lanes].astype(F32)) * silu(z) * valid
        k.out_v[r, :, lanes] = gated.astype(BF16)


def combine(k, pair, seq, rate):
    def one(q, carry):
        d = lax.rem(seq - q + SEQ, SEQ)
        new = []
        for i in range(2):
            k.ret[pair, q, i * 8 : i * 8 + 8, :] = carry[i]
            total = k.recv[pair, d, 16 + i : 17 + i, :]
            new.append(jnp.exp2(rate * total) * carry[i] + k.recv[pair, d, i * 8 : i * 8 + 8, :])
        return tuple(new)

    zero = jnp.zeros((8, 128), F32)
    last = lax.fori_loop(0, SEQ, one, (zero, zero), unroll=2)
    for i in range(2):
        k.final[2 * i + pair] = last[i]


def first_half_token(k, seq, tp, part):
    square = jnp.zeros((8, 128), F32)
    for p in range(SEQ):
        v = k.emb[p].astype(F32)
        square = square + v * v
    scale = lax.rsqrt(jnp.sum(square, axis=1, keepdims=True) / 4096.0 + EPSILON)
    for p in range(SEQ):
        k.nb[:, p * 128 : (p + 1) * 128] = (k.emb[p].astype(F32) * scale).astype(BF16)
    both = lax.dot_general(
        k.nb[...], k.wt_v[...], (((1,), (1,)), ((), ())), preferred_element_type=F32
    )
    both = both.astype(BF16).astype(F32)
    lane = lax.broadcasted_iota(jnp.int32, (8, 128), 1)
    sub = lax.broadcasted_iota(jnp.int32, (8, 128), 0)
    own = (lane // 64 == lax.rem(seq, 2)) & (sub < 3)
    low = jnp.zeros((8, 256), F32)
    bc = jnp.zeros((8, 32), F32)
    for g in range(TP):
        at = lanes_at(g, part)
        x = both[:, g * 64 : g * 64 + 64]
        z = both[:, 256 + g * 64 : 256 + g * 64 + 64]
        t = k.tail[g].astype(F32)
        head = jnp.zeros((4, 128), F32)
        for r in range(TP):
            head = head + jnp.where(tp == r, t[r * 4 : r * 4 + 4], 0.0)
        k.win[0:4, :] = head
        k.win[3:11, :] = jnp.concatenate([x, x], axis=1)
        w = k.cw[:, at].astype(F32)
        acc = k.cb[:, at].astype(F32)
        for tap in range(4):
            acc = acc + w[tap : tap + 1] * k.win[tap : tap + 8, :]
        conv = jnp.where(own, silu(acc), 0.0).astype(BF16)
        low = low + jnp.dot(conv, k.wld_v[g], preferred_element_type=F32)
        bc = bc + lax.dot_general(
            conv, k.wbd_v[g], (((1,), (1,)), ((), ())), preferred_element_type=F32
        )
        k.dc[g] = conv.astype(F32)
        k.dz[g] = jnp.concatenate([z, z], axis=1)
    k.pk[...] = jnp.zeros((16, 128), F32)
    k.pk[0:4, :] = low[0:4, 0:128]
    k.pk[4:8, :] = low[0:4, 128:256]
    k.pk[8:12, 0:32] = bc[0:4]
    k.p_send[...] = k.pk[...].astype(BF16)


def second_half_token(k, seq, part):
    k.pk[...] = jnp.sum(k.p_all[...].astype(F32), axis=0)
    lo = k.pk[0:8, :]
    hi = k.pk[4:12, :]
    bc = k.pk[8:16, :]
    norm = lax.rsqrt(
        (jnp.sum(lo * lo, axis=1, keepdims=True) + jnp.sum(hi * hi, axis=1, keepdims=True)) / 256.0
        + EPSILON
    )
    lane = lax.broadcasted_iota(jnp.int32, (8, 128), 1)
    squares = bc * bc
    b_ms = jnp.sum(jnp.where(lane < NST, squares, 0.0), axis=1, keepdims=True) / NST
    c_ms = (
        jnp.sum(jnp.where((lane >= NST) & (lane < 2 * NST), squares, 0.0), axis=1, keepdims=True)
        / NST
    )
    bc = bc * jnp.where(lane < NST, lax.rsqrt(b_ms + EPSILON), lax.rsqrt(c_ms + EPSILON))
    bct = jnp.transpose(bc)
    lo = (lo * norm).astype(BF16)
    hi = (hi * norm).astype(BF16)
    half = lax.rem(seq, 2)
    sub = lax.broadcasted_iota(jnp.int32, (8, 128), 0)
    parts = []
    for g in range(TP):
        at = lanes_at(g, part)
        v = jnp.dot(lo, k.wpd_v[g, 0:128, :], preferred_element_type=F32)
        v = v + jnp.dot(hi, k.wpd_v[g, 128:256, :], preferred_element_type=F32)
        dt = softplus(v + k.bias[:, at])
        x = k.dc[g]
        u = dt * x
        y = jnp.zeros((8, 128), F32)
        for nh in range(2):
            rate = -jnp.exp(k.ad_v[g, nh * 8 : nh * 8 + 8, :]) * LOG2E
            st = k.fin[g * 2 + nh]
            for j in range(3):
                b = jnp.broadcast_to(bct[nh * 8 : nh * 8 + 8, j : j + 1], (8, 128))
                c = jnp.broadcast_to(bct[NST + nh * 8 : NST + nh * 8 + 8, j : j + 1], (8, 128))
                st = jnp.exp2(rate * dt[j : j + 1]) * st + u[j : j + 1] * b
                y = y + jnp.where(sub == j, jnp.sum(st * c, axis=0, keepdims=True), 0.0)
        gated = ((y + k.skip[:, at] * x) * silu(k.dz[g])).astype(BF16).astype(F32)
        parts.append(jnp.where(half == 1, gated[:, 64:128], gated[:, 0:64]).astype(BF16))
    for p in range(0, SEQ, 4):
        total = jnp.zeros((8, 512), F32)
        for g in range(TP):
            total = total + jnp.dot(
                parts[g], k.ow_v[g, :, p * 128 : p * 128 + 512], preferred_element_type=F32
            )
        for i in range(4):
            k.obuf[p + i] = total[:, i * 128 : i * 128 + 128]


def whole_kernel(names, *refs):
    k = Refs()
    for name, ref in zip(names, refs, strict=True):
        setattr(k, name, ref)
    seq = lax.axis_index("seq")
    tp = lax.axis_index("tp")
    core = lax.rem(tp, 2)
    mate = tp + 1 - 2 * core
    across = lax.rem(tp + 2, TP)
    part = seq // 2
    nh = lax.rem(seq, 2)
    other = 1 - 2 * nh
    base = pl.multiple_of(tp * CH, CH)

    def local(src, dst, sem):
        cp = pltpu.make_async_copy(src, dst, sem)
        cp.start()
        return cp

    x_loads = [local(k.x_hbm.at[r], k.x_v.at[r], k.lsem.at[r]) for r in range(ROWS)]
    wl_load = local(k.wl_hbm.at[pl.ds(base, CH), :], k.wl_v, k.lsem.at[4])
    wb_load = local(k.wb_hbm.at[:, pl.ds(base, CH)], k.wb_v, k.lsem.at[5])
    k.emb_load = local(k.emb_hbm, k.emb_v, k.lsem.at[6])

    barrier = pltpu.get_barrier_semaphore()

    def greet(dseq, dtp):
        pl.semaphore_signal(barrier, inc=1, device_id=(dseq, dtp), device_id_type=MESH)

    for_peers(seq, lambda d, peer: greet(peer, tp))
    for e in range(1, TP):
        greet(seq, lax.rem(tp + e, TP))
        greet(seq + other, lax.rem(tp + e, TP))
    token_terms(k, seq, tp)
    pl.semaphore_wait(barrier, SEQ - 1 + 2 * (TP - 1))

    halo_copy = remote(
        k.x_hbm.at[:, pl.ds(TOK - 16, 16), :], k.halo, k.hsem.at[0], k.hsem.at[1],
        lax.rem(seq + 1, SEQ), tp,
    )
    halo_copy.start()
    e_copies = []
    for e in range(1, TP):
        peer = lax.rem(tp + e, TP)
        cp = remote(k.e_s.at[peer], k.e_recv.at[e], k.asem.at[e], k.asem.at[TP + e], seq, peer)
        cp.start()
        e_copies.append(cp)
    late = [
        local(k.wp_hbm.at[:, pl.ds(base, CH)], k.wp_v, k.lsem.at[7]),
        local(k.a_hbm.at[:, pl.ds(base, CH)], k.a_v, k.lsem.at[8]),
    ]
    for cp in x_loads:
        cp.wait()
    tail_terms(k, seq)

    def send_tail(d, peer):
        remote(
            k.tsend.at[peer // 2], k.trecv.at[d], k.sems.at[0], k.sems.at[1], peer, tp
        ).start()

    for_peers(seq, send_tail)
    wl_load.wait()
    wb_load.wait()
    halo_copy.wait()
    keep = jnp.where(seq > 0, 1.0, 0.0).astype(F32)
    stage_one = []
    for pair in range(2):
        def conv_one(i, c, pair=pair):
            conv_project(k, 2 * i + pair, base, keep)
            return c

        lax.fori_loop(0, 2, conv_one, 0)
        cp = remote(
            k.low.at[2 - 2 * core + pair], k.rlow.at[pair],
            k.tsem.at[pair], k.tsem.at[2 + pair], seq, mate,
        )
        cp.start()
        stage_one.append(cp)
    z_load = local(k.z_hbm, k.z_v, k.lsem.at[9])
    dec_loads = [
        local(k.wt_hbm, k.wt_v, k.lsem.at[10]),
        local(k.ow_hbm, k.ow_v, k.lsem.at[11]),
    ]
    for g in range(TP):
        at = lanes_at(g, part)
        dec_loads.append(local(k.wl_hbm.at[at, :], k.wld_v.at[g], k.lsem.at[12 + g]))
        dec_loads.append(local(k.wb_hbm.at[:, at], k.wbd_v.at[g], k.lsem.at[16 + g]))
        dec_loads.append(local(k.wp_hbm.at[:, at], k.wpd_v.at[g], k.lsem.at[20 + g]))
        dec_loads.append(local(k.a_hbm.at[:, at], k.ad_v.at[g], k.lsem.at[24 + g]))

    for cp in e_copies:
        cp.wait()
    k.ebuf[...] = (
        (k.e_s[tp].astype(F32) + k.e_recv[1].astype(F32))
        + (k.e_recv[2].astype(F32) + k.e_recv[3].astype(F32))
    ).astype(BF16)

    def send_piece(d, peer):
        remote(k.ebuf.at[peer], k.e2.at[d], k.sems.at[2], k.sems.at[3], peer, tp).start()

    for_peers(seq, send_piece)
    stage_two = []
    for pair in range(2):
        stage_one[pair].wait()
        mine = k.low[2 * core + pair] + k.rlow[pair]
        k.slow[pair] = mine
        k.low_send[pair] = mine.astype(BF16)
        cp = remote(
            k.low_send.at[pair], k.low_recv.at[pair],
            k.tsem.at[4 + pair], k.tsem.at[6 + pair], seq, across,
        )
        cp.start()
        stage_two.append(cp)
    for cp in late:
        cp.wait()
    for s in range(16):
        k.a_s[pl.ds(s, NST, stride=16), :] = -jnp.exp(k.a_v[:, s * 128 : s * 128 + 128]) * LOG2E
    rate = -jnp.exp(
        k.a_v[pl.ds(pl.multiple_of(nh * 8, 8), 8), pl.ds(pl.multiple_of(part * 128, 128), 128)]
    ) * LOG2E
    many = k.trecv.at[pl.ds(1, SEQ - 1)]
    remote(many, many, k.sems.at[0], k.sems.at[1], seq + other, tp).wait()
    k.trecv[0] = k.tsend[part]
    k.tsum[...] = jnp.sum(k.trecv[...].astype(F32), axis=0).astype(BF16)
    k.tail[tp] = k.tsum[...]
    t_copies = []
    for e in range(1, TP):
        cp = remote(
            k.tsum, k.tail.at[tp], k.usem.at[e], k.usem.at[TP + e], seq, lax.rem(tp + e, TP)
        )
        cp.start()
        t_copies.append(cp)

    stage_three = []
    for pair in range(2):
        stage_two[pair].wait()
        total = k.slow[pair] + k.low_recv[pair].astype(F32)
        row = 2 * core + pair
        k.dn[row] = rms(total[0:TOK], -1).astype(BF16)
        k.bc[row] = jnp.concatenate(
            [rms(total[TOK:, 0:128], 0), rms(total[TOK:, 128:256], 0)], axis=0
        )
        both = [
            remote(
                k.dn.at[row], k.dn.at[row], k.tsem.at[8 + pair], k.tsem.at[10 + pair], seq, mate
            ),
            remote(
                k.bc.at[row], k.bc.at[row], k.tsem.at[12 + pair], k.tsem.at[14 + pair], seq, mate
            ),
        ]
        for cp in both:
            cp.start()
        stage_three.append(both)
    many_e = k.e2.at[pl.ds(1, SEQ - 1)]
    remote(many_e, many_e, k.sems.at[2], k.sems.at[3], seq + other, tp).wait()
    k.e2[0] = k.ebuf[seq]
    k.esum[...] = jnp.sum(k.e2[...].astype(F32), axis=0).astype(BF16)
    k.emb[seq] = k.esum[...]

    def send_sum(d, peer):
        remote(k.esum, k.emb.at[seq], k.sems.at[4], k.sems.at[5], peer, tp).start()

    for_peers(seq, send_sum)

    def prepare(pair):
        for cp in stage_three[pair]:
            cp.wait()

        def one(i, c):
            spread_columns(k, 2 * i + pair)
            step_sizes(k, 2 * i + pair, seq, base)
            return c

        lax.fori_loop(0, 2, one, 0)

    def send_states(pair):
        def one(d, peer):
            start = pl.multiple_of((lax.rem(peer, 2) * 16 + peer // 2) * 24, 8)
            remote(
                k.send.at[pair, pl.ds(start, 24)], k.recv.at[pair, d],
                k.sems.at[6 + pair], k.sems.at[8 + pair], peer, tp,
            ).start()

        for_peers(seq, one)

    def pass_states(pair):
        lots = k.recv.at[pair, pl.ds(1, SEQ - 1)]
        remote(lots, lots, k.sems.at[6 + pair], k.sems.at[8 + pair], seq + other, tp).wait()
        start = pl.multiple_of((nh * 16 + part) * 24, 8)
        k.recv[pair, 0] = k.send[pair, pl.ds(start, 24), :]
        combine(k, pair, seq, rate)

        def one(d, peer):
            remote(
                k.ret.at[pair, peer], k.inc.at[pair, pl.ds(start, 16)],
                k.sems.at[10 + pair], k.sems.at[12 + pair], peer, tp,
            ).start()

        for_peers(seq, one)
        k.inc[pair, pl.ds(start, 16), :] = k.ret[pair, seq]

    def wait_states(pair):
        lots = k.ret.at[pair, pl.ds(1, SEQ - 1)]
        remote(lots, lots, k.sems.at[10 + pair], k.sems.at[12 + pair], seq + other, tp).wait()

    outs = []

    def finish_row(i, pair):
        r = 2 * i + pair
        pass_two(k, r, pair, i, seq, base)
        outs.append(local(k.out_v.at[r], k.out_hbm.at[r], k.osem.at[r]))

    prepare(0)
    pass_one(k, 0, 0, 0)
    pass_one(k, 2, 0, 1)
    send_states(0)
    many_s = k.emb.at[pl.ds(0, SEQ - 1)]
    remote(many_s, many_s, k.sems.at[4], k.sems.at[5], seq + other, tp).wait()
    for cp in t_copies:
        cp.wait()
    for cp in dec_loads:
        cp.wait()
    first_half_token(k, seq, tp, part)

    def send_p(d, peer):
        remote(k.p_send, k.p_all.at[d], k.sems.at[14], k.sems.at[15], peer, tp).start()

    for_peers(seq, send_p)
    prepare(1)
    pass_states(0)
    pass_one(k, 1, 1, 0)
    pass_one(k, 3, 1, 1)
    send_states(1)
    z_load.wait()
    wait_states(0)
    finish_row(0, 0)
    pass_states(1)
    slot = tp * 2 + nh
    f_copies = []
    for e in range(2):
        for d in range(TP):
            if e == 0 and d == 0:
                continue
            peer_tp = lax.rem(tp + d, TP)
            cp = remote(
                k.final.at[peer_tp], k.fin.at[slot],
                k.fsem.at[e * TP + d], k.fsem.at[8 + e * TP + d], seq + e * other, peer_tp,
            )
            cp.start()
            f_copies.append(cp)
    k.fin[slot] = k.final[tp]
    finish_row(1, 0)
    many_p = k.p_all.at[pl.ds(1, SEQ - 1)]
    remote(many_p, many_p, k.sems.at[14], k.sems.at[15], seq + other, tp).wait()
    k.p_all[0] = k.p_send[...]
    for cp in f_copies:
        cp.wait()
    second_half_token(k, seq, part)

    def send_out(d, peer):
        remote(k.obuf.at[peer], k.orecv.at[d], k.sems.at[16], k.sems.at[17], peer, tp).start()

    for_peers(seq, send_out)
    wait_states(1)
    finish_row(0, 1)
    many_o = k.orecv.at[pl.ds(1, SEQ - 1)]
    remote(many_o, many_o, k.sems.at[16], k.sems.at[17], seq + other, tp).wait()
    k.orecv[0] = k.obuf[seq]
    k.osum[...] = jnp.sum(k.orecv[...], axis=0).astype(BF16)

    def send_total(d, peer):
        remote(k.osum, k.fo.at[seq], k.sems.at[18], k.sems.at[19], peer, tp).start()

    for_peers(seq, send_total)
    k.fo[seq] = k.osum[...]
    finish_row(1, 1)
    many_t = k.fo.at[pl.ds(0, SEQ - 1)]
    remote(many_t, many_t, k.sems.at[18], k.sems.at[19], seq + other, tp).wait()
    for p in range(SEQ):
        k.dec_out[:, p * 128 : (p + 1) * 128] = k.fo[p].astype(F32)[0:3].astype(BF16)
    for cp in outs:
        cp.wait()


INPUTS = (
    ("len", SM), ("ids", SM), ("cw", VM), ("cb", VM), ("bias", VM), ("skip", VM),
    ("x_hbm", ANY), ("z_hbm", ANY), ("wl_hbm", ANY), ("wb_hbm", ANY), ("wp_hbm", ANY),
    ("a_hbm", ANY), ("emb_hbm", ANY), ("wt_hbm", ANY), ("ow_hbm", ANY),
)
SCRATCH = (
    ("x_v", (ROWS, TOK, CH), BF16), ("z_v", (ROWS, TOK, CH), BF16), ("xc", (ROWS, TOK, CH), BF16),
    ("out_v", (ROWS, TOK, CH), BF16), ("wl_v", (CH, 256), BF16), ("wb_v", (32, CH), BF16),
    ("wp_v", (256, CH), BF16), ("a_v", (NST, CH), F32), ("a_s", (256, 128), F32),
    ("emb_v", (512, 4096), BF16), ("wt_v", (512, 4096), BF16), ("ow_v", (TP, 64, 4096), BF16),
    ("wld_v", (TP, 128, 256), BF16), ("wbd_v", (TP, 32, 128), BF16),
    ("wpd_v", (TP, 256, 128), BF16), ("ad_v", (TP, NST, 128), F32),
    ("halo", (ROWS, 16, CH), BF16), ("xp", (16 + TOK, 512), F32),
    ("low", (ROWS, TOK + 16, 256), F32), ("rlow", (2, TOK + 16, 256), F32),
    ("slow", (2, TOK + 16, 256), F32), ("low_send", (2, TOK + 16, 256), BF16),
    ("low_recv", (2, TOK + 16, 256), BF16), ("dn", (ROWS, TOK, 256), BF16),
    ("bc", (ROWS, 32, TOK), F32), ("bcl", (ROWS, TOK * 32, 128), F32),
    ("dt", (ROWS, 16 * PITCH, 128), F32), ("u", (ROWS, 16 * PITCH, 128), F32),
    ("y_s", (16 * PITCH, 128), F32), ("send", (2, SEQ * 24, 128), F32),
    ("recv", (2, SEQ, 24, 128), F32), ("ret", (2, SEQ, 16, 128), F32),
    ("inc", (2, SEQ * 24, 128), F32), ("final", (ROWS, 8, 128), F32), ("fin", (8, 8, 128), F32),
    ("e_s", (ROWS, SEQ, 8, 128), BF16), ("e_recv", (TP, SEQ, 8, 128), BF16),
    ("ebuf", (SEQ, 8, 128), BF16), ("e2", (SEQ, 8, 128), BF16), ("esum", (8, 128), BF16),
    ("emb", (SEQ, 8, 128), BF16), ("tsend", (16, 16, 128), BF16), ("trecv", (SEQ, 16, 128), BF16),
    ("tsum", (16, 128), BF16), ("tail", (TP, 16, 128), BF16), ("nb", (8, 4096), BF16),
    ("win", (16, 128), F32), ("pk", (16, 128), F32), ("p_send", (16, 128), BF16),
    ("p_all", (SEQ, 16, 128), BF16), ("dc", (TP, 8, 128), F32), ("dz", (TP, 8, 128), F32),
    ("obuf", (SEQ, 8, 128), F32), ("orecv", (SEQ, 8, 128), F32), ("osum", (8, 128), BF16),
    ("fo", (SEQ, 8, 128), BF16),
)
SEMS = (
    ("lsem", 28), ("hsem", 2), ("asem", 8), ("tsem", 16), ("usem", 8), ("fsem", 16), ("osem", 4),
    ("sems", 20),
)


def shards(
    x_part, z_part, conv_weight, conv_bias, dt_in_weight, bc_weight, dt_proj, dt_bias, a_log,
    d_skip, lengths, token_ids, embedding, dec_in_weight, out_weight,
):
    names = (
        tuple(name for name, _ in INPUTS) + ("out_hbm", "dec_out")
        + tuple(name for name, _, _ in SCRATCH) + tuple(name for name, _ in SEMS)
    )
    mixed_out, decoded = pl.pallas_call(
        partial(whole_kernel, names),
        out_shape=(
            jax.ShapeDtypeStruct((ROWS, TOK, CH), BF16),
            jax.ShapeDtypeStruct((3, 4096), BF16),
        ),
        in_specs=[spec for _, spec in INPUTS],
        out_specs=(ANY, VM),
        scratch_shapes=[pltpu.VMEM(shape, dtype) for _, shape, dtype in SCRATCH]
        + [pltpu.SemaphoreType.DMA((count,)) for _, count in SEMS],
        compiler_params=pltpu.CompilerParams(
            collective_id=0, has_side_effects=True, vmem_limit_bytes=VLIM
        ),
        name="mixer",
    )(
        lengths, token_ids, conv_weight, conv_bias.reshape(1, -1), dt_bias.reshape(1, -1),
        d_skip.reshape(1, -1), x_part, z_part, dt_in_weight, bc_weight.T, dt_proj, a_log,
        embedding, jnp.transpose(dec_in_weight, (0, 2, 3, 1)).reshape(512, 4096), out_weight,
    )
    return (mixed_out, decoded.reshape(3, 1, 4096))


def solution(mesh):
    return jax.shard_map(
        shards,
        mesh=mesh,
        in_specs=(
            P(None, "seq", "tp"), P(None, "seq", "tp"), P(), P(), P(), P(), P(), P(), P(), P(),
            P(), P(), P(("seq", "tp"), None), P(None, None, None, "seq"), P(None, "seq", None),
        ),
        out_specs=(P(None, "seq", "tp"), P(None, "tp", None)),
        check_vma=False,
    )
```

```python
from functools import partial

import jax
import jax.numpy as jnp
from jax import lax
from jax.experimental import pallas as pl
from jax.experimental.pallas import tpu as pltpu
from jax.sharding import PartitionSpec as P

EPSILON = 1e-06
LOG2E = 1.4426950408889634
MESH = pl.DeviceIdType.MESH
F32 = jnp.float32
BF16 = jnp.bfloat16
SEQ = 32
TP = 4
ROWS = 4
TOK = 128
CH = 2048
NST = 16
ANY = pl.BlockSpec(memory_space=pl.ANY)
VM = pl.BlockSpec(memory_space=pltpu.VMEM)
SM = pl.BlockSpec(memory_space=pltpu.SMEM)
VLIM = 60 * 1024 * 1024


def rms(values, axis):
    return values * lax.rsqrt(jnp.mean(values * values, axis=axis, keepdims=True) + EPSILON)


def silu(values):
    return values * jax.nn.sigmoid(values)


def softplus(values):
    return jnp.maximum(values, 0.0) + jnp.log1p(jnp.exp(-jnp.abs(values)))


def remote(src, dst, send, recv, seq, tp):
    return pltpu.make_async_remote_copy(
        src_ref=src, dst_ref=dst, send_sem=send, recv_sem=recv,
        device_id=(seq, tp), device_id_type=MESH,
    )

PITCH = 136
UNROLL = 16


def for_peers(seq, fn):
    def one(d, c):
        fn(d, lax.rem(seq + d, SEQ))
        return c

    lax.fori_loop(1, SEQ, one, 0)


class Refs:
    pass


def lanes_at(g, part):
    return pl.ds(pl.multiple_of(g * CH + part * 128, 128), 128)


def token_terms(k, seq, tp):
    row = lax.broadcasted_iota(jnp.int32, (32, 512), 0)
    ids = jnp.full((32, 512), -1, jnp.int32)
    for j in range(3):
        for r in range(ROWS):
            ids = jnp.where(row == r * 8 + j, k.ids[j, r], ids)
    here = (seq * TP + tp) * 512 + lax.broadcasted_iota(jnp.int32, (32, 512), 1)
    hot = jnp.where(ids == here, 1.0, 0.0).astype(BF16)
    k.emb_load.wait()
    for p in range(0, SEQ, 4):
        res = jnp.dot(hot, k.emb_v[:, p * 128 : p * 128 + 512], preferred_element_type=F32)
        for r in range(ROWS):
            for i in range(4):
                k.e_s[r, p + i] = res[r * 8 : r * 8 + 8, i * 128 : i * 128 + 128].astype(BF16)


def edge_terms(k, seq):
    token = lax.broadcasted_iota(jnp.int32, (32, TOK), 1)
    pos = seq * TOK + token
    row = lax.broadcasted_iota(jnp.int32, (32, TOK), 0)
    picks = []
    for r in range(ROWS):
        hit = (row == pos - k.len[r] + 3 + 4 * r) & (row >= 4 * r) & (row < 4 * r + 3)
        edge = (row == token - 125 + 16 + 4 * r) & (token >= 125)
        picks.append(jnp.where(hit | edge, 1.0, 0.0).astype(BF16))
    for s in range(0, 16, 4):
        lanes = pl.ds(s * 128, 512)
        tail = jnp.dot(picks[0], k.x_v[0, :, lanes], preferred_element_type=F32)
        for r in range(1, ROWS):
            tail = tail + jnp.dot(picks[r], k.x_v[r, :, lanes], preferred_element_type=F32)
        tail = tail.astype(BF16)
        for i in range(4):
            k.tsend[s + i] = tail[0:16, i * 128 : i * 128 + 128]
        k.hsend[:, lanes] = tail[16:32]


def bias_of(k, first, count):
    return jnp.concatenate([k.cbf[pl.ds(first + i, 1), :] for i in range(count)], axis=1)


def conv_main(k, r, tp, base):
    def chunk(ch, c):
        lanes = pl.ds(pl.multiple_of(ch * 256, 256), 256)
        wide = pl.ds(pl.multiple_of(base + ch * 256, 256), 256)
        k.xp[16 : 16 + TOK, :] = k.x_v[r, :, lanes].astype(F32)
        w = k.cw[:, wide].astype(F32)
        acc = bias_of(k, tp * 16 + ch * 2, 2) + w[0:1] * k.xp[13 : 13 + TOK, :]
        for tap in range(1, 4):
            acc = acc + w[tap : tap + 1] * k.xp[13 + tap : 13 + tap + TOK, :]
        k.xc[r, :, lanes] = silu(acc).astype(BF16)
        return c

    lax.fori_loop(0, 8, chunk, 0)


def conv_edge(k, pair, tp, base, keep):
    def chunk(ch, c):
        lanes = pl.ds(pl.multiple_of(ch * 512, 512), 512)
        wide = pl.ds(pl.multiple_of(base + ch * 512, 512), 512)
        w = k.cw[:, wide].astype(F32)
        bias = bias_of(k, tp * 16 + ch * 4, 4)
        before = k.halo[:, lanes].astype(F32) * keep
        for i in range(2):
            r = 2 * i + pair
            k.xe[i, 5:8, :] = before[4 * r : 4 * r + 3]
            k.xe[i, 8:24, :] = k.x_v[r, 0:16, lanes].astype(F32)
            acc = bias + w[0:1] * k.xe[i, 5:21, :]
            for tap in range(1, 4):
                acc = acc + w[tap : tap + 1] * k.xe[i, 5 + tap : 21 + tap, :]
            k.xc[r, 0:16, lanes] = silu(acc).astype(BF16)
        return c

    lax.fori_loop(0, 4, chunk, 0)


def project(k, r):
    xr = k.xc[r]
    k.low[r, 0:TOK, :] = jnp.dot(xr, k.wl_v[...], preferred_element_type=F32)
    bct = lax.dot_general(k.wb_v[...], xr, (((1,), (1,)), ((), ())), preferred_element_type=F32)
    k.low[r, TOK : TOK + 16, 0:128] = bct[0:NST]
    k.low[r, TOK : TOK + 16, 128:256] = bct[NST:]


def spread_columns(k, r):
    bc = k.bc[r]
    for t in range(TOK):
        k.bcl[r, t * 32 : t * 32 + 32, :] = jnp.broadcast_to(bc[:, t : t + 1], (32, 128))


def step_sizes(k, r, seq, base):
    pos = seq * TOK + lax.broadcasted_iota(jnp.int32, (TOK, 128), 0)
    valid = jnp.where(pos < k.len[r], 1.0, 0.0)
    dn = k.dn[r]
    for s in range(0, 16, 2):
        v2 = jnp.dot(dn, k.wp_v[:, s * 128 : s * 128 + 256], preferred_element_type=F32)
        for i in range(2):
            lanes = pl.ds((s + i) * 128, 128)
            v = v2[:, i * 128 : i * 128 + 128]
            v = v + k.bias[:, pl.ds(pl.multiple_of(base + (s + i) * 128, 128), 128)]
            dt = softplus(v) * valid
            k.dt[r, (s + i) * PITCH : (s + i) * PITCH + TOK, :] = dt
            k.u[r, (s + i) * PITCH : (s + i) * PITCH + TOK, :] = dt * k.xc[r, :, lanes].astype(F32)


def pass_one(k, r, pair, i):
    for half in range(2):
        rates = [k.a_s[n * 16 + half * 8 : n * 16 + half * 8 + 8, :] for n in range(NST)]

        def step(t, carry):
            at = pl.ds(half * 8 * PITCH + t, 8, stride=PITCH)
            dt = k.dt[r, at, :]
            u = k.u[r, at, :]
            new = [carry[0] + dt]
            for n in range(NST):
                b = k.bcl[r, pl.ds(t * 32 + n, 8, stride=0), :]
                new.append(jnp.exp2(dt * rates[n]) * carry[n + 1] + u * b)
            return tuple(new)

        zero = jnp.zeros((8, 128), F32)
        out = lax.fori_loop(0, TOK, step, (zero,) * (NST + 1), unroll=UNROLL)
        for nh in range(2):
            start = (nh * 16 + half * 8) * 24
            k.send[pair, pl.ds(start + 16 + i, 8, stride=24), :] = out[0]
            for n in range(8):
                k.send[pair, pl.ds(start + i * 8 + n, 8, stride=24), :] = out[1 + nh * 8 + n]


def pass_two(k, r, pair, i, seq, base):
    for half in range(2):
        rates = [k.a_s[n * 16 + half * 8 : n * 16 + half * 8 + 8, :] for n in range(NST)]

        def step(t, hs):
            at = pl.ds(half * 8 * PITCH + t, 8, stride=PITCH)
            dt = k.dt[r, at, :]
            u = k.u[r, at, :]
            new = []
            sums = [None] * 4
            for n in range(NST):
                b = k.bcl[r, pl.ds(t * 32 + n, 8, stride=0), :]
                c = k.bcl[r, pl.ds(t * 32 + NST + n, 8, stride=0), :]
                h = jnp.exp2(dt * rates[n]) * hs[n] + u * b
                new.append(h)
                term = h * c
                sums[n % 4] = term if sums[n % 4] is None else sums[n % 4] + term
            k.y_s[at, :] = (sums[0] + sums[1]) + (sums[2] + sums[3])
            return tuple(new)

        first = []
        for n in range(NST):
            start = (n // 8 * 16 + half * 8) * 24 + i * 8 + n % 8
            first.append(k.inc[pair, pl.ds(start, 8, stride=24), :])
        lax.fori_loop(0, TOK, step, tuple(first), unroll=UNROLL)
    pos = seq * TOK + lax.broadcasted_iota(jnp.int32, (TOK, 128), 0)
    valid = jnp.where(pos < k.len[r], 1.0, 0.0)
    for s in range(16):
        lanes = pl.ds(s * 128, 128)
        y = k.y_s[s * PITCH : s * PITCH + TOK, :]
        skip = k.skip[:, pl.ds(pl.multiple_of(base + s * 128, 128), 128)]
        z = k.z_v[r, :, lanes].astype(F32)
        gated = (y + skip * k.xc[r, :, lanes].astype(F32)) * silu(z) * valid
        k.out_v[r, :, lanes] = gated.astype(BF16)


def combine(k, pair, seq, rate):
    def one(q, carry):
        d = lax.rem(seq - q + SEQ, SEQ)
        new = []
        for i in range(2):
            k.ret[pair, q, i * 8 : i * 8 + 8, :] = carry[i]
            total = k.recv[pair, d, 16 + i : 17 + i, :]
            new.append(jnp.exp2(rate * total) * carry[i] + k.recv[pair, d, i * 8 : i * 8 + 8, :])
        return tuple(new)

    zero = jnp.zeros((8, 128), F32)
    last = lax.fori_loop(0, SEQ, one, (zero, zero), unroll=2)
    for i in range(2):
        k.final[2 * i + pair] = last[i]


def first_half_token(k, seq, tp, part):
    square = jnp.zeros((8, 128), F32)
    for p in range(SEQ):
        v = k.emb[p].astype(F32)
        square = square + v * v
    scale = lax.rsqrt(jnp.sum(square, axis=1, keepdims=True) / 4096.0 + EPSILON)
    for p in range(SEQ):
        k.nb[:, p * 128 : (p + 1) * 128] = (k.emb[p].astype(F32) * scale).astype(BF16)
    both = lax.dot_general(
        k.nb[...], k.wt_v[...], (((1,), (1,)), ((), ())), preferred_element_type=F32
    )
    both = both.astype(BF16).astype(F32)
    lane = lax.broadcasted_iota(jnp.int32, (8, 128), 1)
    sub = lax.broadcasted_iota(jnp.int32, (8, 128), 0)
    own = (lane // 64 == lax.rem(seq, 2)) & (sub < 3)
    low = jnp.zeros((8, 256), F32)
    bc = jnp.zeros((8, 32), F32)
    for g in range(TP):
        at = lanes_at(g, part)
        x = both[:, g * 64 : g * 64 + 64]
        z = both[:, 256 + g * 64 : 256 + g * 64 + 64]
        t = k.tail[g].astype(F32)
        head = jnp.zeros((4, 128), F32)
        for r in range(TP):
            head = head + jnp.where(tp == r, t[r * 4 : r * 4 + 4], 0.0)
        k.win[0:4, :] = head
        k.win[3:11, :] = jnp.concatenate([x, x], axis=1)
        w = k.cw[:, at].astype(F32)
        acc = k.cbf[pl.ds(g * 16 + part, 1), :]
        for tap in range(4):
            acc = acc + w[tap : tap + 1] * k.win[tap : tap + 8, :]
        conv = jnp.where(own, silu(acc), 0.0).astype(BF16)
        low = low + jnp.dot(conv, k.wld_v[g], preferred_element_type=F32)
        bc = bc + lax.dot_general(
            conv, k.wbd_v[g], (((1,), (1,)), ((), ())), preferred_element_type=F32
        )
        k.dc[g] = conv.astype(F32)
        k.dz[g] = jnp.concatenate([z, z], axis=1)
    k.pk[...] = jnp.zeros((16, 128), F32)
    k.pk[0:4, :] = low[0:4, 0:128]
    k.pk[4:8, :] = low[0:4, 128:256]
    k.pk[8:12, 0:32] = bc[0:4]
    k.p_send[...] = k.pk[...].astype(BF16)


def second_half_token(k, seq, part):
    k.pk[...] = jnp.sum(k.p_all[...].astype(F32), axis=0)
    lo = k.pk[0:8, :]
    hi = k.pk[4:12, :]
    bc = k.pk[8:16, :]
    norm = lax.rsqrt(
        (jnp.sum(lo * lo, axis=1, keepdims=True) + jnp.sum(hi * hi, axis=1, keepdims=True)) / 256.0
        + EPSILON
    )
    lane = lax.broadcasted_iota(jnp.int32, (8, 128), 1)
    squares = bc * bc
    b_ms = jnp.sum(jnp.where(lane < NST, squares, 0.0), axis=1, keepdims=True) / NST
    c_ms = (
        jnp.sum(jnp.where((lane >= NST) & (lane < 2 * NST), squares, 0.0), axis=1, keepdims=True)
        / NST
    )
    bc = bc * jnp.where(lane < NST, lax.rsqrt(b_ms + EPSILON), lax.rsqrt(c_ms + EPSILON))
    bct = jnp.transpose(bc)
    lo = (lo * norm).astype(BF16)
    hi = (hi * norm).astype(BF16)
    half = lax.rem(seq, 2)
    sub = lax.broadcasted_iota(jnp.int32, (8, 128), 0)
    parts = []
    for g in range(TP):
        at = lanes_at(g, part)
        v = jnp.dot(lo, k.wpd_v[g, 0:128, :], preferred_element_type=F32)
        v = v + jnp.dot(hi, k.wpd_v[g, 128:256, :], preferred_element_type=F32)
        dt = softplus(v + k.bias[:, at])
        x = k.dc[g]
        u = dt * x
        y = jnp.zeros((8, 128), F32)
        for nh in range(2):
            rate = -jnp.exp(k.ad_v[g, nh * 8 : nh * 8 + 8, :]) * LOG2E
            st = k.fin[g * 2 + nh]
            for j in range(3):
                b = jnp.broadcast_to(bct[nh * 8 : nh * 8 + 8, j : j + 1], (8, 128))
                c = jnp.broadcast_to(bct[NST + nh * 8 : NST + nh * 8 + 8, j : j + 1], (8, 128))
                st = jnp.exp2(rate * dt[j : j + 1]) * st + u[j : j + 1] * b
                y = y + jnp.where(sub == j, jnp.sum(st * c, axis=0, keepdims=True), 0.0)
        gated = ((y + k.skip[:, at] * x) * silu(k.dz[g])).astype(BF16).astype(F32)
        parts.append(jnp.where(half == 1, gated[:, 64:128], gated[:, 0:64]).astype(BF16))
    for p in range(0, SEQ, 4):
        total = jnp.zeros((8, 512), F32)
        for g in range(TP):
            total = total + jnp.dot(
                parts[g], k.ow_v[g, :, p * 128 : p * 128 + 512], preferred_element_type=F32
            )
        for i in range(4):
            k.obuf[p + i] = total[:, i * 128 : i * 128 + 128]


def whole_kernel(names, *refs):
    k = Refs()
    for name, ref in zip(names, refs, strict=True):
        setattr(k, name, ref)
    seq = lax.axis_index("seq")
    tp = lax.axis_index("tp")
    core = lax.rem(tp, 2)
    mate = tp + 1 - 2 * core
    across = lax.rem(tp + 2, TP)
    part = seq // 2
    nh = lax.rem(seq, 2)
    other = 1 - 2 * nh
    base = pl.multiple_of(tp * CH, CH)

    def local(src, dst, sem):
        cp = pltpu.make_async_copy(src, dst, sem)
        cp.start()
        return cp

    x_loads = [local(k.x_hbm.at[r], k.x_v.at[r], k.lsem.at[r]) for r in range(ROWS)]
    barrier = pltpu.get_barrier_semaphore()

    def greet(dseq, dtp):
        pl.semaphore_signal(barrier, inc=1, device_id=(dseq, dtp), device_id_type=MESH)

    for_peers(seq, lambda d, peer: greet(peer, tp))
    for e in range(1, TP):
        greet(seq, lax.rem(tp + e, TP))
        greet(seq + other, lax.rem(tp + e, TP))
    k.cbf[...] = k.cb[...].astype(F32)
    for cp in x_loads:
        cp.wait()
    k.emb_load = local(k.emb_hbm, k.emb_v, k.lsem.at[6])
    wl_load = local(k.wl_hbm.at[pl.ds(base, CH), :], k.wl_v, k.lsem.at[4])
    wb_load = local(k.wb_hbm.at[:, pl.ds(base, CH)], k.wb_v, k.lsem.at[5])
    edge_terms(k, seq)
    conv_main(k, 0, tp, base)
    conv_main(k, 2, tp, base)
    pl.semaphore_wait(barrier, SEQ - 1 + 2 * (TP - 1))
    halo_copy = remote(
        k.hsend, k.halo, k.hsem.at[0], k.hsem.at[1], lax.rem(seq + 1, SEQ), tp
    )
    halo_copy.start()
    token_terms(k, seq, tp)
    e_copies = []
    for e in range(1, TP):
        peer = lax.rem(tp + e, TP)
        cp = remote(k.e_s.at[peer], k.e_recv.at[e], k.asem.at[e], k.asem.at[TP + e], seq, peer)
        cp.start()
        e_copies.append(cp)
    late = [
        local(k.wp_hbm.at[:, pl.ds(base, CH)], k.wp_v, k.lsem.at[7]),
        local(k.a_hbm.at[:, pl.ds(base, CH)], k.a_v, k.lsem.at[8]),
    ]

    def send_tail(d, peer):
        remote(
            k.tsend.at[peer // 2], k.trecv.at[d], k.sems.at[0], k.sems.at[1], peer, tp
        ).start()

    for_peers(seq, send_tail)
    wl_load.wait()
    wb_load.wait()
    conv_main(k, 1, tp, base)
    halo_copy.wait()
    keep = jnp.where(seq > 0, 1.0, 0.0).astype(F32)

    def start_one(pair):
        conv_edge(k, pair, tp, base, keep)

        def one(i, c):
            project(k, 2 * i + pair)
            return c

        lax.fori_loop(0, 2, one, 0)
        cp = remote(
            k.low.at[2 - 2 * core + pair], k.rlow.at[pair],
            k.tsem.at[pair], k.tsem.at[2 + pair], seq, mate,
        )
        cp.start()
        return cp

    def start_two(pair, first):
        first.wait()
        mine = k.low[2 * core + pair] + k.rlow[pair]
        k.slow[pair] = mine
        k.low_send[pair] = mine.astype(BF16)
        cp = remote(
            k.low_send.at[pair], k.low_recv.at[pair],
            k.tsem.at[4 + pair], k.tsem.at[6 + pair], seq, across,
        )
        cp.start()
        return cp

    def start_three(pair, second):
        second.wait()
        total = k.slow[pair] + k.low_recv[pair].astype(F32)
        row = 2 * core + pair
        k.dn[row] = rms(total[0:TOK], -1).astype(BF16)
        k.bc[row] = jnp.concatenate(
            [rms(total[TOK:, 0:128], 0), rms(total[TOK:, 128:256], 0)], axis=0
        )
        both = [
            remote(
                k.dn.at[row], k.dn.at[row], k.tsem.at[8 + pair], k.tsem.at[10 + pair], seq, mate
            ),
            remote(
                k.bc.at[row], k.bc.at[row], k.tsem.at[12 + pair], k.tsem.at[14 + pair], seq, mate
            ),
        ]
        for cp in both:
            cp.start()
        return both

    one_a = start_one(0)
    conv_main(k, 3, tp, base)
    two_a = start_two(0, one_a)
    one_b = start_one(1)
    for cp in e_copies:
        cp.wait()
    k.ebuf[...] = (
        (k.e_s[tp].astype(F32) + k.e_recv[1].astype(F32))
        + (k.e_recv[2].astype(F32) + k.e_recv[3].astype(F32))
    ).astype(BF16)

    def send_piece(d, peer):
        remote(k.ebuf.at[peer], k.e2.at[d], k.sems.at[2], k.sems.at[3], peer, tp).start()

    for_peers(seq, send_piece)
    two_b = start_two(1, one_b)
    for cp in late:
        cp.wait()
    for s in range(16):
        k.a_s[pl.ds(s, NST, stride=16), :] = -jnp.exp(k.a_v[:, s * 128 : s * 128 + 128]) * LOG2E
    rate = -jnp.exp(
        k.a_v[pl.ds(pl.multiple_of(nh * 8, 8), 8), pl.ds(pl.multiple_of(part * 128, 128), 128)]
    ) * LOG2E
    many = k.trecv.at[pl.ds(1, SEQ - 1)]
    remote(many, many, k.sems.at[0], k.sems.at[1], seq + other, tp).wait()
    k.trecv[0] = k.tsend[part]
    k.tsum[...] = jnp.sum(k.trecv[...].astype(F32), axis=0).astype(BF16)
    k.tail[tp] = k.tsum[...]
    t_copies = []
    for e in range(1, TP):
        cp = remote(
            k.tsum, k.tail.at[tp], k.usem.at[e], k.usem.at[TP + e], seq, lax.rem(tp + e, TP)
        )
        cp.start()
        t_copies.append(cp)

    three_a = start_three(0, two_a)
    z_load = local(k.z_hbm, k.z_v, k.lsem.at[9])
    dec_loads = [
        local(k.wt_hbm, k.wt_v, k.lsem.at[10]),
        local(k.ow_hbm, k.ow_v, k.lsem.at[11]),
    ]
    for g in range(TP):
        at = lanes_at(g, part)
        dec_loads.append(local(k.wl_hbm.at[at, :], k.wld_v.at[g], k.lsem.at[12 + g]))
        dec_loads.append(local(k.wb_hbm.at[:, at], k.wbd_v.at[g], k.lsem.at[16 + g]))
        dec_loads.append(local(k.wp_hbm.at[:, at], k.wpd_v.at[g], k.lsem.at[20 + g]))
        dec_loads.append(local(k.a_hbm.at[:, at], k.ad_v.at[g], k.lsem.at[24 + g]))
    def prepare(pair, copies):
        for cp in copies:
            cp.wait()

        def one(i, c):
            spread_columns(k, 2 * i + pair)
            step_sizes(k, 2 * i + pair, seq, base)
            return c

        lax.fori_loop(0, 2, one, 0)

    def send_states(pair):
        def one(d, peer):
            start = pl.multiple_of((lax.rem(peer, 2) * 16 + peer // 2) * 24, 8)
            remote(
                k.send.at[pair, pl.ds(start, 24)], k.recv.at[pair, d],
                k.sems.at[6 + pair], k.sems.at[8 + pair], peer, tp,
            ).start()

        for_peers(seq, one)

    def pass_states(pair):
        lots = k.recv.at[pair, pl.ds(1, SEQ - 1)]
        remote(lots, lots, k.sems.at[6 + pair], k.sems.at[8 + pair], seq + other, tp).wait()
        start = pl.multiple_of((nh * 16 + part) * 24, 8)
        k.recv[pair, 0] = k.send[pair, pl.ds(start, 24), :]
        combine(k, pair, seq, rate)

        def one(d, peer):
            remote(
                k.ret.at[pair, peer], k.inc.at[pair, pl.ds(start, 16)],
                k.sems.at[10 + pair], k.sems.at[12 + pair], peer, tp,
            ).start()

        for_peers(seq, one)
        k.inc[pair, pl.ds(start, 16), :] = k.ret[pair, seq]

    def wait_states(pair):
        lots = k.ret.at[pair, pl.ds(1, SEQ - 1)]
        remote(lots, lots, k.sems.at[10 + pair], k.sems.at[12 + pair], seq + other, tp).wait()

    outs = []

    def finish_row(i, pair):
        r = 2 * i + pair
        pass_two(k, r, pair, i, seq, base)
        outs.append(local(k.out_v.at[r], k.out_hbm.at[r], k.osem.at[r]))

    prepare(0, three_a)
    three_b = start_three(1, two_b)
    many_e = k.e2.at[pl.ds(1, SEQ - 1)]
    remote(many_e, many_e, k.sems.at[2], k.sems.at[3], seq + other, tp).wait()
    k.e2[0] = k.ebuf[seq]
    k.esum[...] = jnp.sum(k.e2[...].astype(F32), axis=0).astype(BF16)
    k.emb[seq] = k.esum[...]

    def send_sum(d, peer):
        remote(k.esum, k.emb.at[seq], k.sems.at[4], k.sems.at[5], peer, tp).start()

    for_peers(seq, send_sum)
    pass_one(k, 0, 0, 0)
    pass_one(k, 2, 0, 1)
    send_states(0)
    many_s = k.emb.at[pl.ds(0, SEQ - 1)]
    remote(many_s, many_s, k.sems.at[4], k.sems.at[5], seq + other, tp).wait()
    for cp in t_copies:
        cp.wait()
    for cp in dec_loads:
        cp.wait()
    first_half_token(k, seq, tp, part)

    def send_p(d, peer):
        remote(k.p_send, k.p_all.at[d], k.sems.at[14], k.sems.at[15], peer, tp).start()

    for_peers(seq, send_p)
    prepare(1, three_b)
    pass_states(0)
    pass_one(k, 1, 1, 0)
    pass_one(k, 3, 1, 1)
    send_states(1)
    z_load.wait()
    wait_states(0)
    finish_row(0, 0)
    pass_states(1)
    slot = tp * 2 + nh
    f_copies = []
    for e in range(2):
        for d in range(TP):
            if e == 0 and d == 0:
                continue
            peer_tp = lax.rem(tp + d, TP)
            cp = remote(
                k.final.at[peer_tp], k.fin.at[slot],
                k.fsem.at[e * TP + d], k.fsem.at[8 + e * TP + d], seq + e * other, peer_tp,
            )
            cp.start()
            f_copies.append(cp)
    k.fin[slot] = k.final[tp]
    finish_row(1, 0)
    many_p = k.p_all.at[pl.ds(1, SEQ - 1)]
    remote(many_p, many_p, k.sems.at[14], k.sems.at[15], seq + other, tp).wait()
    k.p_all[0] = k.p_send[...]
    for cp in f_copies:
        cp.wait()
    second_half_token(k, seq, part)

    def send_out(d, peer):
        remote(k.obuf.at[peer], k.orecv.at[d], k.sems.at[16], k.sems.at[17], peer, tp).start()

    for_peers(seq, send_out)
    wait_states(1)
    finish_row(0, 1)
    many_o = k.orecv.at[pl.ds(1, SEQ - 1)]
    remote(many_o, many_o, k.sems.at[16], k.sems.at[17], seq + other, tp).wait()
    k.orecv[0] = k.obuf[seq]
    k.osum[...] = jnp.sum(k.orecv[...], axis=0).astype(BF16)

    def send_total(d, peer):
        remote(k.osum, k.fo.at[seq], k.sems.at[18], k.sems.at[19], peer, tp).start()

    for_peers(seq, send_total)
    k.fo[seq] = k.osum[...]
    finish_row(1, 1)
    many_t = k.fo.at[pl.ds(0, SEQ - 1)]
    remote(many_t, many_t, k.sems.at[18], k.sems.at[19], seq + other, tp).wait()
    for p in range(SEQ):
        k.dec_out[:, p * 128 : (p + 1) * 128] = k.fo[p].astype(F32)[0:3].astype(BF16)
    for cp in outs:
        cp.wait()


INPUTS = (
    ("len", SM), ("ids", SM), ("cw", VM), ("cb", VM), ("bias", VM), ("skip", VM),
    ("x_hbm", ANY), ("z_hbm", ANY), ("wl_hbm", ANY), ("wb_hbm", ANY), ("wp_hbm", ANY),
    ("a_hbm", ANY), ("emb_hbm", ANY), ("wt_hbm", ANY), ("ow_hbm", ANY),
)
SCRATCH = (
    ("x_v", (ROWS, TOK, CH), BF16), ("z_v", (ROWS, TOK, CH), BF16), ("xc", (ROWS, TOK, CH), BF16),
    ("out_v", (ROWS, TOK, CH), BF16), ("wl_v", (CH, 256), BF16), ("wb_v", (32, CH), BF16),
    ("wp_v", (256, CH), BF16), ("a_v", (NST, CH), F32), ("a_s", (256, 128), F32),
    ("emb_v", (512, 4096), BF16), ("wt_v", (512, 4096), BF16), ("ow_v", (TP, 64, 4096), BF16),
    ("wld_v", (TP, 128, 256), BF16), ("wbd_v", (TP, 32, 128), BF16),
    ("wpd_v", (TP, 256, 128), BF16), ("ad_v", (TP, NST, 128), F32),
    ("halo", (16, CH), BF16), ("hsend", (16, CH), BF16), ("cbf", (64, 128), F32),
    ("xp", (16 + TOK, 256), F32), ("xe", (2, 24, 512), F32),
    ("low", (ROWS, TOK + 16, 256), F32), ("rlow", (2, TOK + 16, 256), F32),
    ("slow", (2, TOK + 16, 256), F32), ("low_send", (2, TOK + 16, 256), BF16),
    ("low_recv", (2, TOK + 16, 256), BF16), ("dn", (ROWS, TOK, 256), BF16),
    ("bc", (ROWS, 32, TOK), F32), ("bcl", (ROWS, TOK * 32, 128), F32),
    ("dt", (ROWS, 16 * PITCH, 128), F32), ("u", (ROWS, 16 * PITCH, 128), F32),
    ("y_s", (16 * PITCH, 128), F32), ("send", (2, SEQ * 24, 128), F32),
    ("recv", (2, SEQ, 24, 128), F32), ("ret", (2, SEQ, 16, 128), F32),
    ("inc", (2, SEQ * 24, 128), F32), ("final", (ROWS, 8, 128), F32), ("fin", (8, 8, 128), F32),
    ("e_s", (ROWS, SEQ, 8, 128), BF16), ("e_recv", (TP, SEQ, 8, 128), BF16),
    ("ebuf", (SEQ, 8, 128), BF16), ("e2", (SEQ, 8, 128), BF16), ("esum", (8, 128), BF16),
    ("emb", (SEQ, 8, 128), BF16), ("tsend", (16, 16, 128), BF16), ("trecv", (SEQ, 16, 128), BF16),
    ("tsum", (16, 128), BF16), ("tail", (TP, 16, 128), BF16), ("nb", (8, 4096), BF16),
    ("win", (16, 128), F32), ("pk", (16, 128), F32), ("p_send", (16, 128), BF16),
    ("p_all", (SEQ, 16, 128), BF16), ("dc", (TP, 8, 128), F32), ("dz", (TP, 8, 128), F32),
    ("obuf", (SEQ, 8, 128), F32), ("orecv", (SEQ, 8, 128), F32), ("osum", (8, 128), BF16),
    ("fo", (SEQ, 8, 128), BF16),
)
SEMS = (
    ("lsem", 28), ("hsem", 2), ("asem", 8), ("tsem", 16), ("usem", 8), ("fsem", 16), ("osem", 4),
    ("sems", 20),
)


def shards(
    x_part, z_part, conv_weight, conv_bias, dt_in_weight, bc_weight, dt_proj, dt_bias, a_log,
    d_skip, lengths, token_ids, embedding, dec_in_weight, out_weight,
):
    names = (
        tuple(name for name, _ in INPUTS) + ("out_hbm", "dec_out")
        + tuple(name for name, _, _ in SCRATCH) + tuple(name for name, _ in SEMS)
    )
    mixed_out, decoded = pl.pallas_call(
        partial(whole_kernel, names),
        out_shape=(
            jax.ShapeDtypeStruct((ROWS, TOK, CH), BF16),
            jax.ShapeDtypeStruct((3, 4096), BF16),
        ),
        in_specs=[spec for _, spec in INPUTS],
        out_specs=(ANY, VM),
        scratch_shapes=[pltpu.VMEM(shape, dtype) for _, shape, dtype in SCRATCH]
        + [pltpu.SemaphoreType.DMA((count,)) for _, count in SEMS],
        compiler_params=pltpu.CompilerParams(
            collective_id=0, has_side_effects=True, vmem_limit_bytes=VLIM
        ),
        name="mixer",
    )(
        lengths, token_ids, conv_weight, conv_bias.reshape(64, 128), dt_bias.reshape(1, -1),
        d_skip.reshape(1, -1), x_part, z_part, dt_in_weight, bc_weight.T, dt_proj, a_log,
        embedding, jnp.transpose(dec_in_weight, (0, 2, 3, 1)).reshape(512, 4096), out_weight,
    )
    return (mixed_out, decoded.reshape(3, 1, 4096))


def solution(mesh):
    return jax.shard_map(
        shards,
        mesh=mesh,
        in_specs=(
            P(None, "seq", "tp"), P(None, "seq", "tp"), P(), P(), P(), P(), P(), P(), P(), P(),
            P(), P(), P(("seq", "tp"), None), P(None, None, None, "seq"), P(None, "seq", None),
        ),
        out_specs=(P(None, "seq", "tp"), P(None, "tp", None)),
        check_vma=False,
    )
```

```python
from functools import partial

import jax
import jax.numpy as jnp
from jax import lax
from jax.experimental import pallas as pl
from jax.experimental.pallas import tpu as pltpu
from jax.sharding import PartitionSpec as P

EPSILON = 1e-06
LOG2E = 1.4426950408889634
MESH = pl.DeviceIdType.MESH
F32 = jnp.float32
BF16 = jnp.bfloat16
SEQ = 32
TP = 4
ROWS = 4
TOK = 128
CH = 2048
NST = 16
HBM = pl.BlockSpec(memory_space=pltpu.HBM)
VM = pl.BlockSpec(memory_space=pltpu.VMEM)
SM = pl.BlockSpec(memory_space=pltpu.SMEM)
VLIM = 60 * 1024 * 1024


def rms(values, axis):
    return values * lax.rsqrt(jnp.mean(values * values, axis=axis, keepdims=True) + EPSILON)


def silu(values):
    return values * jax.nn.sigmoid(values)


def softplus(values):
    return jnp.maximum(values, 0.0) + jnp.log1p(jnp.exp(-jnp.abs(values)))


def remote(src, dst, send, recv, seq, tp):
    return pltpu.make_async_remote_copy(
        src_ref=src, dst_ref=dst, send_sem=send, recv_sem=recv,
        device_id=(seq, tp), device_id_type=MESH,
    )

PITCH = 136
UNROLL = 16


def for_peers(seq, fn):
    def one(d, c):
        fn(d, lax.rem(seq + d, SEQ))
        return c

    lax.fori_loop(1, SEQ, one, 0)


class Refs:
    pass


def lanes_at(g, part):
    return pl.ds(pl.multiple_of(g * CH + part * 128, 128), 128)


def token_terms(k, seq, tp):
    row = lax.broadcasted_iota(jnp.int32, (32, 512), 0)
    ids = jnp.full((32, 512), -1, jnp.int32)
    for j in range(3):
        for r in range(ROWS):
            ids = jnp.where(row == r * 8 + j, k.ids[j, r], ids)
    here = (seq * TP + tp) * 512 + lax.broadcasted_iota(jnp.int32, (32, 512), 1)
    hot = jnp.where(ids == here, 1.0, 0.0).astype(BF16)
    k.emb_load.wait()
    for p in range(0, SEQ, 4):
        res = jnp.dot(hot, k.emb_v[:, p * 128 : p * 128 + 512], preferred_element_type=F32)
        for r in range(ROWS):
            for i in range(4):
                k.e_s[r, p + i] = res[r * 8 : r * 8 + 8, i * 128 : i * 128 + 128].astype(BF16)


def edge_terms(k, seq):
    token = lax.broadcasted_iota(jnp.int32, (32, TOK), 1)
    pos = seq * TOK + token
    row = lax.broadcasted_iota(jnp.int32, (32, TOK), 0)
    picks = []
    for r in range(ROWS):
        hit = (row == pos - k.len[r] + 3 + 4 * r) & (row >= 4 * r) & (row < 4 * r + 3)
        edge = (row == token - 125 + 16 + 4 * r) & (token >= 125)
        picks.append(jnp.where(hit | edge, 1.0, 0.0).astype(BF16))
    for s in range(0, 16, 4):
        lanes = pl.ds(s * 128, 512)
        tail = jnp.dot(picks[0], k.x_v[0, :, lanes], preferred_element_type=F32)
        for r in range(1, ROWS):
            tail = tail + jnp.dot(picks[r], k.x_v[r, :, lanes], preferred_element_type=F32)
        tail = tail.astype(BF16)
        for i in range(4):
            k.tsend[s + i] = tail[0:16, i * 128 : i * 128 + 128]
        k.hsend[:, lanes] = tail[16:32]


def bias_of(k, first, count):
    return jnp.concatenate([k.cbf[pl.ds(first + i, 1), :] for i in range(count)], axis=1)


def conv_main(k, r, tp, base):
    def chunk(ch, c):
        lanes = pl.ds(pl.multiple_of(ch * 128, 128), 128)
        wide = pl.ds(pl.multiple_of(base + ch * 128, 128), 128)
        k.xp[16 : 16 + TOK, :] = k.x_v[r, :, lanes].astype(F32)
        w = k.cw[:, wide].astype(F32)
        acc = bias_of(k, tp * 16 + ch, 1) + w[0:1] * k.xp[13 : 13 + TOK, :]
        for tap in range(1, 4):
            acc = acc + w[tap : tap + 1] * k.xp[13 + tap : 13 + tap + TOK, :]
        k.xc[r, :, lanes] = silu(acc).astype(BF16)
        return c

    lax.fori_loop(0, 16, chunk, 0)


def conv_edge(k, pair, tp, base, keep):
    def chunk(ch, c):
        lanes = pl.ds(pl.multiple_of(ch * 512, 512), 512)
        wide = pl.ds(pl.multiple_of(base + ch * 512, 512), 512)
        w = k.cw[:, wide].astype(F32)
        bias = bias_of(k, tp * 16 + ch * 4, 4)
        before = k.halo[:, lanes].astype(F32) * keep
        for i in range(2):
            r = 2 * i + pair
            k.xe[i, 5:8, :] = before[4 * r : 4 * r + 3]
            k.xe[i, 8:24, :] = k.x_v[r, 0:16, lanes].astype(F32)
            acc = bias + w[0:1] * k.xe[i, 5:21, :]
            for tap in range(1, 4):
                acc = acc + w[tap : tap + 1] * k.xe[i, 5 + tap : 21 + tap, :]
            k.xc[r, 0:16, lanes] = silu(acc).astype(BF16)
        return c

    lax.fori_loop(0, 4, chunk, 0)


def project(k, r):
    xr = k.xc[r]
    k.low[r, 0:TOK, :] = jnp.dot(xr, k.wl_v[...], preferred_element_type=F32)
    bct = lax.dot_general(k.wb_v[...], xr, (((1,), (1,)), ((), ())), preferred_element_type=F32)
    k.low[r, TOK : TOK + 16, 0:128] = bct[0:NST]
    k.low[r, TOK : TOK + 16, 128:256] = bct[NST:]


def spread_columns(k, r):
    bc = k.bc[r]
    for t in range(TOK):
        k.bcl[r, t * 32 : t * 32 + 32, :] = jnp.broadcast_to(bc[:, t : t + 1], (32, 128))


def step_sizes(k, r, seq, base):
    pos = seq * TOK + lax.broadcasted_iota(jnp.int32, (TOK, 128), 0)
    valid = jnp.where(pos < k.len[r], 1.0, 0.0)
    dn = k.dn[r]
    for s in range(0, 16, 2):
        v2 = jnp.dot(dn, k.wp_v[:, s * 128 : s * 128 + 256], preferred_element_type=F32)
        for i in range(2):
            lanes = pl.ds((s + i) * 128, 128)
            v = v2[:, i * 128 : i * 128 + 128]
            v = v + k.bias[:, pl.ds(pl.multiple_of(base + (s + i) * 128, 128), 128)]
            dt = softplus(v) * valid
            k.dt[r, (s + i) * PITCH : (s + i) * PITCH + TOK, :] = dt
            k.u[r, (s + i) * PITCH : (s + i) * PITCH + TOK, :] = dt * k.xc[r, :, lanes].astype(F32)


def pass_one(k, r, pair, i, keep=False):
    for half in range(2):
        rates = [k.a_s[n * 16 + half * 8 : n * 16 + half * 8 + 8, :] for n in range(NST)]

        def step(t, carry):
            at = pl.ds(half * 8 * PITCH + t, 8, stride=PITCH)
            dt = k.dt[r, at, :]
            u = k.u[r, at, :]
            new = [carry[0] + dt]
            for n in range(NST):
                b = k.bcl[r, pl.ds(t * 32 + n, 8, stride=0), :]
                decay = jnp.exp2(dt * rates[n])
                if keep:
                    k.decays[half, t, n * 8 : n * 8 + 8, :] = decay
                new.append(decay * carry[n + 1] + u * b)
            return tuple(new)

        zero = jnp.zeros((8, 128), F32)
        out = lax.fori_loop(0, TOK, step, (zero,) * (NST + 1), unroll=UNROLL)
        for nh in range(2):
            start = (nh * 16 + half * 8) * 24
            k.send[pair, pl.ds(start + 16 + i, 8, stride=24), :] = out[0]
            for n in range(8):
                k.send[pair, pl.ds(start + i * 8 + n, 8, stride=24), :] = out[1 + nh * 8 + n]


def pass_two(k, r, pair, i, seq, base, kept=False):
    for half in range(2):
        rates = [k.a_s[n * 16 + half * 8 : n * 16 + half * 8 + 8, :] for n in range(NST)]

        def step(t, hs):
            at = pl.ds(half * 8 * PITCH + t, 8, stride=PITCH)
            dt = k.dt[r, at, :]
            u = k.u[r, at, :]
            new = []
            sums = [None] * 4
            for n in range(NST):
                b = k.bcl[r, pl.ds(t * 32 + n, 8, stride=0), :]
                c = k.bcl[r, pl.ds(t * 32 + NST + n, 8, stride=0), :]
                if kept:
                    decay = k.decays[half, t, n * 8 : n * 8 + 8, :]
                else:
                    decay = jnp.exp2(dt * rates[n])
                h = decay * hs[n] + u * b
                new.append(h)
                term = h * c
                sums[n % 4] = term if sums[n % 4] is None else sums[n % 4] + term
            k.y_s[at, :] = (sums[0] + sums[1]) + (sums[2] + sums[3])
            return tuple(new)

        first = []
        for n in range(NST):
            start = (n // 8 * 16 + half * 8) * 24 + i * 8 + n % 8
            first.append(k.inc[pair, pl.ds(start, 8, stride=24), :])
        lax.fori_loop(0, TOK, step, tuple(first), unroll=UNROLL)
    for s in range(16):
        lanes = pl.ds(s * 128, 128)
        y = k.y_s[s * PITCH : s * PITCH + TOK, :]
        skip = k.skip[:, pl.ds(pl.multiple_of(base + s * 128, 128), 128)]
        z = k.z_v[r, :, lanes].astype(F32)
        gated = (y + skip * k.xc[r, :, lanes].astype(F32)) * z
        k.x_v[r, :, lanes] = gated.astype(BF16)


def gate_factors(k, seq):
    def one(r, c):
        pos = seq * TOK + lax.broadcasted_iota(jnp.int32, (TOK, 128), 0)
        valid = jnp.where(pos < k.len[r], 1.0, 0.0)
        for s in range(16):
            lanes = pl.ds(s * 128, 128)
            k.z_v[r, :, lanes] = (silu(k.z_v[r, :, lanes].astype(F32)) * valid).astype(BF16)
        return c

    lax.fori_loop(0, ROWS, one, 0)


def combine(k, pair, seq, rate):
    def one(q, carry):
        d = lax.rem(seq - q + SEQ, SEQ)
        new = []
        for i in range(2):
            k.ret[pair, q, i * 8 : i * 8 + 8, :] = carry[i]
            total = k.recv[pair, d, 16 + i : 17 + i, :]
            new.append(jnp.exp2(rate * total) * carry[i] + k.recv[pair, d, i * 8 : i * 8 + 8, :])
        return tuple(new)

    zero = jnp.zeros((8, 128), F32)
    last = lax.fori_loop(0, SEQ, one, (zero, zero), unroll=2)
    for i in range(2):
        k.final[2 * i + pair] = last[i]


def first_half_token(k, seq, tp, part):
    square = jnp.zeros((8, 128), F32)
    for p in range(SEQ):
        v = k.emb[p].astype(F32)
        square = square + v * v
    scale = lax.rsqrt(jnp.sum(square, axis=1, keepdims=True) / 4096.0 + EPSILON)
    for p in range(SEQ):
        k.nb[:, p * 128 : (p + 1) * 128] = (k.emb[p].astype(F32) * scale).astype(BF16)
    both = lax.dot_general(
        k.nb[...], k.wt_v[...], (((1,), (1,)), ((), ())), preferred_element_type=F32
    )
    both = both.astype(BF16).astype(F32)
    lane = lax.broadcasted_iota(jnp.int32, (8, 128), 1)
    sub = lax.broadcasted_iota(jnp.int32, (8, 128), 0)
    own = (lane // 64 == lax.rem(seq, 2)) & (sub < 3)
    low = jnp.zeros((8, 256), F32)
    bc = jnp.zeros((8, 32), F32)
    for g in range(TP):
        at = lanes_at(g, part)
        x = both[:, g * 64 : g * 64 + 64]
        z = both[:, 256 + g * 64 : 256 + g * 64 + 64]
        t = k.tail[g].astype(F32)
        head = jnp.zeros((4, 128), F32)
        for r in range(TP):
            head = head + jnp.where(tp == r, t[r * 4 : r * 4 + 4], 0.0)
        k.win[0:4, :] = head
        k.win[3:11, :] = jnp.concatenate([x, x], axis=1)
        w = k.cw[:, at].astype(F32)
        acc = k.cbf[pl.ds(g * 16 + part, 1), :]
        for tap in range(4):
            acc = acc + w[tap : tap + 1] * k.win[tap : tap + 8, :]
        conv = jnp.where(own, silu(acc), 0.0).astype(BF16)
        low = low + jnp.dot(conv, k.wld_v[g], preferred_element_type=F32)
        bc = bc + lax.dot_general(
            conv, k.wbd_v[g], (((1,), (1,)), ((), ())), preferred_element_type=F32
        )
        k.dc[g] = conv.astype(F32)
        k.dz[g] = jnp.concatenate([z, z], axis=1)
    k.pk[...] = jnp.zeros((16, 128), F32)
    k.pk[0:4, :] = low[0:4, 0:128]
    k.pk[4:8, :] = low[0:4, 128:256]
    k.pk[8:12, 0:32] = bc[0:4]
    k.p_send[...] = k.pk[...].astype(BF16)


def second_half_token(k, seq, part):
    k.pk[...] = jnp.sum(k.p_all[...].astype(F32), axis=0)
    lo = k.pk[0:8, :]
    hi = k.pk[4:12, :]
    bc = k.pk[8:16, :]
    norm = lax.rsqrt(
        (jnp.sum(lo * lo, axis=1, keepdims=True) + jnp.sum(hi * hi, axis=1, keepdims=True)) / 256.0
        + EPSILON
    )
    lane = lax.broadcasted_iota(jnp.int32, (8, 128), 1)
    squares = bc * bc
    b_ms = jnp.sum(jnp.where(lane < NST, squares, 0.0), axis=1, keepdims=True) / NST
    c_ms = (
        jnp.sum(jnp.where((lane >= NST) & (lane < 2 * NST), squares, 0.0), axis=1, keepdims=True)
        / NST
    )
    bc = bc * jnp.where(lane < NST, lax.rsqrt(b_ms + EPSILON), lax.rsqrt(c_ms + EPSILON))
    bct = jnp.transpose(bc)
    lo = (lo * norm).astype(BF16)
    hi = (hi * norm).astype(BF16)
    half = lax.rem(seq, 2)
    sub = lax.broadcasted_iota(jnp.int32, (8, 128), 0)
    parts = []
    for g in range(TP):
        at = lanes_at(g, part)
        v = jnp.dot(lo, k.wpd_v[g, 0:128, :], preferred_element_type=F32)
        v = v + jnp.dot(hi, k.wpd_v[g, 128:256, :], preferred_element_type=F32)
        dt = softplus(v + k.bias[:, at])
        x = k.dc[g]
        u = dt * x
        y = jnp.zeros((8, 128), F32)
        for nh in range(2):
            rate = -jnp.exp(k.ad_v[g, nh * 8 : nh * 8 + 8, :]) * LOG2E
            st = k.fin[g * 2 + nh]
            for j in range(3):
                b = jnp.broadcast_to(bct[nh * 8 : nh * 8 + 8, j : j + 1], (8, 128))
                c = jnp.broadcast_to(bct[NST + nh * 8 : NST + nh * 8 + 8, j : j + 1], (8, 128))
                st = jnp.exp2(rate * dt[j : j + 1]) * st + u[j : j + 1] * b
                y = y + jnp.where(sub == j, jnp.sum(st * c, axis=0, keepdims=True), 0.0)
        gated = ((y + k.skip[:, at] * x) * silu(k.dz[g])).astype(BF16).astype(F32)
        parts.append(jnp.where(half == 1, gated[:, 64:128], gated[:, 0:64]).astype(BF16))
    for p in range(0, SEQ, 4):
        total = jnp.zeros((8, 512), F32)
        for g in range(TP):
            total = total + jnp.dot(
                parts[g], k.ow_v[g, :, p * 128 : p * 128 + 512], preferred_element_type=F32
            )
        for i in range(4):
            k.obuf[p + i] = total[:, i * 128 : i * 128 + 128]


def whole_kernel(names, *refs):
    k = Refs()
    for name, ref in zip(names, refs, strict=True):
        setattr(k, name, ref)
    seq = lax.axis_index("seq")
    tp = lax.axis_index("tp")
    core = lax.rem(tp, 2)
    mate = tp + 1 - 2 * core
    across = lax.rem(tp + 2, TP)
    part = seq // 2
    nh = lax.rem(seq, 2)
    other = 1 - 2 * nh
    base = pl.multiple_of(tp * CH, CH)

    def local(src, dst, sem):
        cp = pltpu.make_async_copy(src, dst, sem)
        cp.start()
        return cp

    x_loads = [local(k.x_hbm.at[r], k.x_v.at[r], k.lsem.at[r]) for r in range(ROWS)]
    barrier = pltpu.get_barrier_semaphore()

    def greet(dseq, dtp):
        pl.semaphore_signal(barrier, inc=1, device_id=(dseq, dtp), device_id_type=MESH)

    for_peers(seq, lambda d, peer: greet(peer, tp))
    for e in range(1, TP):
        greet(seq, lax.rem(tp + e, TP))
        greet(seq + other, lax.rem(tp + e, TP))
    k.cbf[...] = k.cb[...].astype(F32)
    for cp in x_loads:
        cp.wait()
    k.emb_load = local(k.emb_hbm, k.emb_v, k.lsem.at[6])
    z_load = local(k.z_hbm, k.z_v, k.lsem.at[9])
    wl_load = local(k.wl_hbm.at[pl.ds(base, CH), :], k.wl_v, k.lsem.at[4])
    wb_load = local(k.wb_hbm.at[:, pl.ds(base, CH)], k.wb_v, k.lsem.at[5])
    edge_terms(k, seq)
    conv_main(k, 0, tp, base)
    conv_main(k, 2, tp, base)
    pl.semaphore_wait(barrier, SEQ - 1 + 2 * (TP - 1))
    halo_copy = remote(
        k.hsend, k.halo, k.hsem.at[0], k.hsem.at[1], lax.rem(seq + 1, SEQ), tp
    )
    halo_copy.start()
    token_terms(k, seq, tp)
    e_copies = []
    for e in range(1, TP):
        peer = lax.rem(tp + e, TP)
        cp = remote(k.e_s.at[peer], k.e_recv.at[e], k.asem.at[e], k.asem.at[TP + e], seq, peer)
        cp.start()
        e_copies.append(cp)
    late = [
        local(k.wp_hbm.at[:, pl.ds(base, CH)], k.wp_v, k.lsem.at[7]),
        local(k.a_hbm.at[:, pl.ds(base, CH)], k.a_v, k.lsem.at[8]),
    ]

    def send_tail(d, peer):
        remote(
            k.tsend.at[peer // 2], k.trecv.at[d], k.sems.at[0], k.sems.at[1], peer, tp
        ).start()

    for_peers(seq, send_tail)
    wl_load.wait()
    wb_load.wait()
    conv_main(k, 1, tp, base)
    z_load.wait()
    gate_factors(k, seq)
    halo_copy.wait()
    keep = jnp.where(seq > 0, 1.0, 0.0).astype(F32)

    def start_one(pair):
        conv_edge(k, pair, tp, base, keep)

        def one(i, c):
            project(k, 2 * i + pair)
            return c

        lax.fori_loop(0, 2, one, 0)
        cp = remote(
            k.low.at[2 - 2 * core + pair], k.rlow.at[pair],
            k.tsem.at[pair], k.tsem.at[2 + pair], seq, mate,
        )
        cp.start()
        return cp

    def start_two(pair, first):
        first.wait()
        mine = k.low[2 * core + pair] + k.rlow[pair]
        k.slow[pair] = mine
        k.low_send[pair] = mine.astype(BF16)
        cp = remote(
            k.low_send.at[pair], k.low_recv.at[pair],
            k.tsem.at[4 + pair], k.tsem.at[6 + pair], seq, across,
        )
        cp.start()
        return cp

    def start_three(pair, second):
        second.wait()
        total = k.slow[pair] + k.low_recv[pair].astype(F32)
        row = 2 * core + pair
        k.dn[row] = rms(total[0:TOK], -1).astype(BF16)
        k.bc[row] = jnp.concatenate(
            [rms(total[TOK:, 0:128], 0), rms(total[TOK:, 128:256], 0)], axis=0
        )
        both = [
            remote(
                k.dn.at[row], k.dn.at[row], k.tsem.at[8 + pair], k.tsem.at[10 + pair], seq, mate
            ),
            remote(
                k.bc.at[row], k.bc.at[row], k.tsem.at[12 + pair], k.tsem.at[14 + pair], seq, mate
            ),
        ]
        for cp in both:
            cp.start()
        return both

    one_a = start_one(0)
    conv_main(k, 3, tp, base)
    two_a = start_two(0, one_a)
    one_b = start_one(1)
    for cp in e_copies:
        cp.wait()
    k.ebuf[...] = (
        (k.e_s[tp].astype(F32) + k.e_recv[1].astype(F32))
        + (k.e_recv[2].astype(F32) + k.e_recv[3].astype(F32))
    ).astype(BF16)

    def send_piece(d, peer):
        remote(k.ebuf.at[peer], k.e2.at[d], k.sems.at[2], k.sems.at[3], peer, tp).start()

    for_peers(seq, send_piece)
    two_b = start_two(1, one_b)
    for cp in late:
        cp.wait()
    for s in range(16):
        k.a_s[pl.ds(s, NST, stride=16), :] = -jnp.exp(k.a_v[:, s * 128 : s * 128 + 128]) * LOG2E
    rate = -jnp.exp(
        k.a_v[pl.ds(pl.multiple_of(nh * 8, 8), 8), pl.ds(pl.multiple_of(part * 128, 128), 128)]
    ) * LOG2E
    many = k.trecv.at[pl.ds(1, SEQ - 1)]
    remote(many, many, k.sems.at[0], k.sems.at[1], seq + other, tp).wait()
    k.trecv[0] = k.tsend[part]
    k.tsum[...] = jnp.sum(k.trecv[...].astype(F32), axis=0).astype(BF16)
    k.tail[tp] = k.tsum[...]
    t_copies = []
    for e in range(1, TP):
        cp = remote(
            k.tsum, k.tail.at[tp], k.usem.at[e], k.usem.at[TP + e], seq, lax.rem(tp + e, TP)
        )
        cp.start()
        t_copies.append(cp)

    three_a = start_three(0, two_a)
    dec_loads = [
        local(k.wt_hbm, k.wt_v, k.lsem.at[10]),
        local(k.ow_hbm, k.ow_v, k.lsem.at[11]),
    ]
    for g in range(TP):
        at = lanes_at(g, part)
        dec_loads.append(local(k.wl_hbm.at[at, :], k.wld_v.at[g], k.lsem.at[12 + g]))
        dec_loads.append(local(k.wb_hbm.at[:, at], k.wbd_v.at[g], k.lsem.at[16 + g]))
        dec_loads.append(local(k.wp_hbm.at[:, at], k.wpd_v.at[g], k.lsem.at[20 + g]))
        dec_loads.append(local(k.a_hbm.at[:, at], k.ad_v.at[g], k.lsem.at[24 + g]))
    def prepare(pair, copies):
        for cp in copies:
            cp.wait()

        def one(i, c):
            spread_columns(k, 2 * i + pair)
            step_sizes(k, 2 * i + pair, seq, base)
            return c

        lax.fori_loop(0, 2, one, 0)

    def send_states(pair):
        def one(d, peer):
            start = pl.multiple_of((lax.rem(peer, 2) * 16 + peer // 2) * 24, 8)
            remote(
                k.send.at[pair, pl.ds(start, 24)], k.recv.at[pair, d],
                k.sems.at[6 + pair], k.sems.at[8 + pair], peer, tp,
            ).start()

        for_peers(seq, one)

    def pass_states(pair):
        lots = k.recv.at[pair, pl.ds(1, SEQ - 1)]
        remote(lots, lots, k.sems.at[6 + pair], k.sems.at[8 + pair], seq + other, tp).wait()
        start = pl.multiple_of((nh * 16 + part) * 24, 8)
        k.recv[pair, 0] = k.send[pair, pl.ds(start, 24), :]
        combine(k, pair, seq, rate)

        def one(d, peer):
            remote(
                k.ret.at[pair, peer], k.inc.at[pair, pl.ds(start, 16)],
                k.sems.at[10 + pair], k.sems.at[12 + pair], peer, tp,
            ).start()

        for_peers(seq, one)
        k.inc[pair, pl.ds(start, 16), :] = k.ret[pair, seq]

    def wait_states(pair):
        lots = k.ret.at[pair, pl.ds(1, SEQ - 1)]
        remote(lots, lots, k.sems.at[10 + pair], k.sems.at[12 + pair], seq + other, tp).wait()

    outs = []

    def finish_row(i, pair):
        r = 2 * i + pair
        pass_two(k, r, pair, i, seq, base, kept=r == 3)
        outs.append(local(k.x_v.at[r], k.mixed.at[r], k.lsem.at[r]))

    prepare(0, three_a)
    three_b = start_three(1, two_b)
    many_e = k.e2.at[pl.ds(1, SEQ - 1)]
    remote(many_e, many_e, k.sems.at[2], k.sems.at[3], seq + other, tp).wait()
    k.e2[0] = k.ebuf[seq]
    k.esum[...] = jnp.sum(k.e2[...].astype(F32), axis=0).astype(BF16)
    k.emb[seq] = k.esum[...]

    def send_sum(d, peer):
        remote(k.esum, k.emb.at[seq], k.sems.at[4], k.sems.at[5], peer, tp).start()

    for_peers(seq, send_sum)
    pass_one(k, 0, 0, 0)
    pass_one(k, 2, 0, 1)
    send_states(0)
    prepare(1, three_b)
    pass_one(k, 1, 1, 0)
    pass_states(0)
    pass_one(k, 3, 1, 1, keep=True)
    send_states(1)
    many_s = k.emb.at[pl.ds(0, SEQ - 1)]
    remote(many_s, many_s, k.sems.at[4], k.sems.at[5], seq + other, tp).wait()
    for cp in t_copies:
        cp.wait()
    for cp in dec_loads:
        cp.wait()
    first_half_token(k, seq, tp, part)

    def send_p(d, peer):
        remote(k.p_send, k.p_all.at[d], k.sems.at[14], k.sems.at[15], peer, tp).start()

    for_peers(seq, send_p)
    wait_states(0)
    finish_row(0, 0)
    pass_states(1)
    slot = tp * 2 + nh
    f_copies = []
    for e in range(2):
        for d in range(TP):
            if e == 0 and d == 0:
                continue
            peer_tp = lax.rem(tp + d, TP)
            cp = remote(
                k.final.at[peer_tp], k.fin.at[slot],
                k.fsem.at[e * TP + d], k.fsem.at[8 + e * TP + d], seq + e * other, peer_tp,
            )
            cp.start()
            f_copies.append(cp)
    k.fin[slot] = k.final[tp]
    finish_row(1, 0)
    many_p = k.p_all.at[pl.ds(1, SEQ - 1)]
    remote(many_p, many_p, k.sems.at[14], k.sems.at[15], seq + other, tp).wait()
    k.p_all[0] = k.p_send[...]
    for cp in f_copies:
        cp.wait()
    second_half_token(k, seq, part)

    def send_out(d, peer):
        remote(k.obuf.at[peer], k.orecv.at[d], k.sems.at[16], k.sems.at[17], peer, tp).start()

    for_peers(seq, send_out)
    wait_states(1)
    finish_row(0, 1)
    many_o = k.orecv.at[pl.ds(1, SEQ - 1)]
    remote(many_o, many_o, k.sems.at[16], k.sems.at[17], seq + other, tp).wait()
    k.orecv[0] = k.obuf[seq]
    k.osum[...] = jnp.sum(k.orecv[...], axis=0).astype(BF16)

    def send_total(d, peer):
        remote(k.osum, k.fo.at[seq], k.sems.at[18], k.sems.at[19], peer, tp).start()

    for_peers(seq, send_total)
    k.fo[seq] = k.osum[...]
    finish_row(1, 1)
    many_t = k.fo.at[pl.ds(0, SEQ - 1)]
    remote(many_t, many_t, k.sems.at[18], k.sems.at[19], seq + other, tp).wait()
    for p in range(SEQ):
        k.dec_out[:, p * 128 : (p + 1) * 128] = k.fo[p].astype(F32)[0:3].astype(BF16)
    for cp in outs:
        cp.wait()


PIECES = 16


def result_kernel(mixed_ref, decoded_ref, out_ref, dec_ref, held, sem):
    per_row = PIECES // ROWS
    size = TOK // per_row
    loads = []
    for p in range(PIECES):
        cp = pltpu.make_async_copy(mixed_ref.at[p], held.at[p], sem.at[0, p])
        cp.start()
        loads.append(cp)
    dec_ref[...] = decoded_ref[...]
    stores = []
    for p in range(PIECES):
        loads[p].wait()
        cp = pltpu.make_async_copy(
            held.at[p], out_ref.at[p // per_row, pl.ds(p % per_row * size, size), :], sem.at[1, p]
        )
        cp.start()
        stores.append(cp)
    for cp in stores:
        cp.wait()


INPUTS = (
    ("len", SM), ("ids", SM), ("cw", VM), ("cb", VM), ("bias", VM), ("skip", VM),
    ("x_hbm", HBM), ("z_hbm", HBM), ("wl_hbm", HBM), ("wb_hbm", HBM), ("wp_hbm", HBM),
    ("a_hbm", HBM), ("emb_hbm", HBM), ("wt_hbm", HBM), ("ow_hbm", HBM),
)
SCRATCH = (
    ("decays", (2, TOK, 128, 128), F32),
    ("x_v", (ROWS, TOK, CH), BF16), ("z_v", (ROWS, TOK, CH), BF16), ("xc", (ROWS, TOK, CH), BF16),
    ("wl_v", (CH, 256), BF16), ("wb_v", (32, CH), BF16),
    ("wp_v", (256, CH), BF16), ("a_v", (NST, CH), F32), ("a_s", (256, 128), F32),
    ("emb_v", (512, 4096), BF16), ("wt_v", (512, 4096), BF16), ("ow_v", (TP, 64, 4096), BF16),
    ("wld_v", (TP, 128, 256), BF16), ("wbd_v", (TP, 32, 128), BF16),
    ("wpd_v", (TP, 256, 128), BF16), ("ad_v", (TP, NST, 128), F32),
    ("halo", (16, CH), BF16), ("hsend", (16, CH), BF16), ("cbf", (64, 128), F32),
    ("xp", (16 + TOK, 128), F32), ("xe", (2, 24, 512), F32),
    ("low", (ROWS, TOK + 16, 256), F32), ("rlow", (2, TOK + 16, 256), F32),
    ("slow", (2, TOK + 16, 256), F32), ("low_send", (2, TOK + 16, 256), BF16),
    ("low_recv", (2, TOK + 16, 256), BF16), ("dn", (ROWS, TOK, 256), BF16),
    ("bc", (ROWS, 32, TOK), F32), ("bcl", (ROWS, TOK * 32, 128), F32),
    ("dt", (ROWS, 16 * PITCH, 128), F32), ("u", (ROWS, 16 * PITCH, 128), F32),
    ("y_s", (16 * PITCH, 128), F32), ("send", (2, SEQ * 24, 128), F32),
    ("recv", (2, SEQ, 24, 128), F32), ("ret", (2, SEQ, 16, 128), F32),
    ("inc", (2, SEQ * 24, 128), F32), ("final", (ROWS, 8, 128), F32), ("fin", (8, 8, 128), F32),
    ("e_s", (ROWS, SEQ, 8, 128), BF16), ("e_recv", (TP, SEQ, 8, 128), BF16),
    ("ebuf", (SEQ, 8, 128), BF16), ("e2", (SEQ, 8, 128), BF16), ("esum", (8, 128), BF16),
    ("emb", (SEQ, 8, 128), BF16), ("tsend", (16, 16, 128), BF16), ("trecv", (SEQ, 16, 128), BF16),
    ("tsum", (16, 128), BF16), ("tail", (TP, 16, 128), BF16), ("nb", (8, 4096), BF16),
    ("win", (16, 128), F32), ("pk", (16, 128), F32), ("p_send", (16, 128), BF16),
    ("p_all", (SEQ, 16, 128), BF16), ("dc", (TP, 8, 128), F32), ("dz", (TP, 8, 128), F32),
    ("obuf", (SEQ, 8, 128), F32), ("orecv", (SEQ, 8, 128), F32), ("osum", (8, 128), BF16),
    ("fo", (SEQ, 8, 128), BF16),
)
SEMS = (
    ("lsem", 28), ("hsem", 2), ("asem", 8), ("tsem", 16), ("usem", 8), ("fsem", 16), ("sems", 20),
)


def shards(
    x_part, z_part, conv_weight, conv_bias, dt_in_weight, bc_weight, dt_proj, dt_bias, a_log,
    d_skip, lengths, token_ids, embedding, dec_in_weight, out_weight,
):
    names = (
        tuple(name for name, _ in INPUTS) + ("mixed", "dec_out")
        + tuple(name for name, _, _ in SCRATCH) + tuple(name for name, _ in SEMS)
    )
    mixed_out, decoded = pl.pallas_call(
        partial(whole_kernel, names),
        out_shape=(
            jax.ShapeDtypeStruct((ROWS, TOK, CH), BF16),
            jax.ShapeDtypeStruct((3, 4096), BF16),
        ),
        in_specs=[spec for _, spec in INPUTS],
        out_specs=(HBM, VM),
        scratch_shapes=[pltpu.VMEM(shape, dtype) for _, shape, dtype in SCRATCH]
        + [pltpu.SemaphoreType.DMA((count,)) for _, count in SEMS],
        compiler_params=pltpu.CompilerParams(
            collective_id=0, has_side_effects=True, vmem_limit_bytes=VLIM
        ),
        name="mixer",
    )(
        lengths, token_ids, conv_weight, conv_bias.reshape(64, 128), dt_bias.reshape(1, -1),
        d_skip.reshape(1, -1), x_part, z_part, dt_in_weight, bc_weight.T, dt_proj, a_log,
        embedding, jnp.transpose(dec_in_weight, (0, 2, 3, 1)).reshape(512, 4096), out_weight,
    )
    mixed_out, decoded = pl.pallas_call(
        result_kernel,
        out_shape=(
            jax.ShapeDtypeStruct((ROWS, TOK, CH), BF16),
            jax.ShapeDtypeStruct((3, 4096), BF16),
        ),
        in_specs=[HBM, VM],
        out_specs=(HBM, VM),
        scratch_shapes=[
            pltpu.VMEM((PIECES, ROWS * TOK // PIECES, CH), BF16),
            pltpu.SemaphoreType.DMA((2, PIECES)),
        ],
        name="results",
    )(mixed_out.reshape(PIECES, ROWS * TOK // PIECES, CH), decoded)
    return (mixed_out, decoded.reshape(3, 1, 4096))


def solution(mesh):
    return jax.shard_map(
        shards,
        mesh=mesh,
        in_specs=(
            P(None, "seq", "tp"), P(None, "seq", "tp"), P(), P(), P(), P(), P(), P(), P(), P(),
            P(), P(), P(("seq", "tp"), None), P(None, None, None, "seq"), P(None, "seq", None),
        ),
        out_specs=(P(None, "seq", "tp"), P(None, "tp", None)),
        check_vma=False,
    )
```
